256 devices in a mesh: gx: 8 (over x, y_hi), gy: 32 (over y_lo, z, core).
Axes of the slice: x: 4, y: 4 (y_hi: 2, y_lo: 2; y = y_hi * 2 + y_lo), z: 8, core: 2. Of those that a mesh axis runs over, the one named last changes fastest.
Arguments:
- noise: float32 [16, 64, 4, 128], P('gx', 'gy'), may hold values from -4 to 4
- w_first: bfloat16 [16, 1, 3, 3, 3, 3], replicated, may hold values from -0.625 to 0.625
- b_first: float32 [16], replicated, may hold values from -2 to 2
- w_middle: bfloat16 [16, 16, 3, 3, 3, 3], replicated, may hold values from -0.15625 to 0.15625
- b_middle: float32 [16], replicated, may hold values from -2 to 2
- w_last: bfloat16 [2, 16, 3, 3, 3, 3], replicated, may hold values from -0.15625 to 0.15625
- b_last: float32 [2], replicated, may hold values from -2 to 2
Outputs:
- field: float32 [16, 64, 4, 128], P('gx', 'gy')
- noise_grad: float32 [16, 64, 4, 128], P('gx', 'gy')
- loss: float32 [], replicated
- w_first_grad: float32 [16, 1, 3, 3, 3, 3], replicated
- b_first_grad: float32 [16], replicated
- w_middle_grad: float32 [16, 16, 3, 3, 3, 3], replicated
- b_middle_grad: float32 [16], replicated
- w_last_grad: float32 [2, 16, 3, 3, 3, 3], replicated
- b_last_grad: float32 [2], replicated
The draws below stay inside these ranges and needn't reach their ends.
All inputs are finite; a program needn't handle non-finite values.
Results may differ from the reference program's by a relative error of at most 0.0074.
Values may be sent and summed in bfloat16 or wider, within the bound.
No kernel may reach another device: no remote copies, remote signals or barrier semaphores. Data moves between devices by JAX's collectives and lax.ppermute only.
A program may use at most 128 MiB of HBM per device.

```python
import jax
import jax.numpy as jnp
from jax import lax

CH = 16
LT = 4
LZ = 128
LX = 16
LY = 64


def block_scale(stream_key, dims, split, smallest, largest):
    factor_of = 1.0
    for position, parts in split:
        steps = jax.random.uniform(jax.random.fold_in(jax.random.fold_in(stream_key, 6), position), (parts,), jnp.float32, smallest / len(split), largest / len(split))
        factor_of = factor_of * jnp.repeat(jnp.exp(steps), dims[position] // parts).reshape((-1,) + (1,) * (len(dims) - 1 - position))
    return factor_of


def gaussian(stream_key, shape, scale, bound, shards=(), kind=jnp.bfloat16):
    entries = scale * jax.random.normal(stream_key, shape, jnp.float32)
    if shards:
        entries = entries * block_scale(stream_key, shape, shards, -0.22, 0.18)
    return jnp.clip(entries, -bound, bound).astype(kind)


def setup_inputs(seed: int = 0) -> dict:
    splits = jax.random.split(jax.random.key(seed), 8)
    return {
        "noise": gaussian(splits[0], (LX, LY, LT, LZ), 1.0, 4.0, ((0, 8), (1, 32)), jnp.float32),
        "w_first": gaussian(splits[1], (CH, 1, 3, 3, 3, 3), 81 ** -0.5, 0.625),
        "b_first": gaussian(splits[2], (CH,), 0.5, 2.0, (), jnp.float32),
        "w_middle": gaussian(splits[3], (CH, CH, 3, 3, 3, 3), (CH * 81) ** -0.5, 0.15625),
        "b_middle": gaussian(splits[4], (CH,), 0.5, 2.0, (), jnp.float32),
        "w_last": gaussian(splits[5], (2, CH, 3, 3, 3, 3), (CH * 81) ** -0.5, 0.15625),
        "b_last": gaussian(splits[6], (2,), 0.5, 2.0, (), jnp.float32),
    }


HOPPING = 0.15
QUARTIC = 0.1

def parity_mask(shape, offset_x, offset_y):
    index_x = jnp.arange(shape[0], dtype=jnp.int32) + offset_x
    index_y = jnp.arange(shape[1], dtype=jnp.int32) + offset_y
    index_t = jnp.arange(shape[2], dtype=jnp.int32)
    index_z = jnp.arange(shape[3], dtype=jnp.int32)
    summed = index_x[:, None, None, None] + index_y[None, :, None, None] + index_t[None, None, :, None] + index_z[None, None, None, :]
    return jnp.where(summed % 2 == 0, 1.0, 0.0).astype(jnp.float32)

def conv_block(padded, kernel):
    width_x = padded.shape[0] - 2
    width_y = padded.shape[1] - 2
    summed = None
    for a in range(3):
        for b in range(3):
            window = padded[a:a + width_x, b:b + width_y]
            flattened = window.reshape((width_x * width_y,) + window.shape[2:])
            partial_out = lax.conv_general_dilated(flattened, kernel[:, :, a, b], (1, 1), 'VALID', preferred_element_type=jnp.float32)
            summed = partial_out if summed is None else summed + partial_out
    return summed.reshape((width_x, width_y) + summed.shape[1:])

def kernel_grad(padded, cotangent):
    width_x = cotangent.shape[0]
    width_y = cotangent.shape[1]
    flat_cot = cotangent.reshape((width_x * width_y,) + cotangent.shape[2:])
    pieces = []
    for a in range(3):
        for b in range(3):
            window = padded[a:a + width_x, b:b + width_y]
            flattened = window.reshape((width_x * width_y,) + window.shape[2:])
            pieces.append(lax.conv_general_dilated(flattened, flat_cot, (1, 1), 'VALID', dimension_numbers=('CNHW', 'IOHW', 'NCHW'), preferred_element_type=jnp.float32))
    stacked = jnp.stack(pieces).reshape((3, 3) + pieces[0].shape)
    return jnp.transpose(stacked, (3, 2, 0, 1, 4, 5))

def flip_kernel(kernel):
    return jnp.transpose(kernel[:, :, ::-1, ::-1, ::-1, ::-1], (1, 0, 2, 3, 4, 5))

def wrap_all(field):
    return jnp.pad(field, ((1, 1), (1, 1), (0, 0), (1, 1), (1, 1)), mode='wrap')

def channel_bias(bias):
    return bias[None, None, :, None, None]

def reference(noise, w_first, b_first, w_middle, b_middle, w_last, b_last):
    frozen = parity_mask(noise.shape, 0, 0)
    active = 1.0 - frozen
    sites = float(noise.size)
    inputs = (frozen * noise).astype(jnp.bfloat16)[:, :, None]
    hidden_one = jnp.tanh(conv_block(wrap_all(inputs), w_first) + channel_bias(b_first)).astype(jnp.bfloat16)
    hidden_two = jnp.tanh(conv_block(wrap_all(hidden_one), w_middle) + channel_bias(b_middle)).astype(jnp.bfloat16)
    head_out = conv_block(wrap_all(hidden_two), w_last) + channel_bias(b_last)
    log_scale = jnp.tanh(head_out[:, :, 0])
    offset_field = head_out[:, :, 1]
    growth = jnp.exp(log_scale)
    field = frozen * noise + active * (noise * growth + offset_field)
    upward = jnp.roll(field, -1, 0) + jnp.roll(field, -1, 1) + jnp.roll(field, -1, 2) + jnp.roll(field, -1, 3)
    downward = jnp.roll(field, 1, 0) + jnp.roll(field, 1, 1) + jnp.roll(field, 1, 2) + jnp.roll(field, 1, 3)
    squared = field * field
    density = -2.0 * HOPPING * field * upward + squared + QUARTIC * (squared - 1.0) * (squared - 1.0)
    summed = jnp.sum(-0.5 * noise * noise - active * log_scale + density)
    force_field = -2.0 * HOPPING * (upward + downward) + 2.0 * field + 4.0 * QUARTIC * field * (squared - 1.0)
    d_scale = active * (force_field * noise * growth - 1.0) * (1.0 - log_scale * log_scale)
    d_offset = active * force_field
    cot_last = jnp.stack([d_scale, d_offset], axis=2).astype(jnp.bfloat16)
    grad_last = kernel_grad(wrap_all(hidden_two), cot_last)
    bias_last = lax.optimization_barrier(jnp.sum(cot_last.astype(jnp.float32), axis=(0, 1, 3, 4)))
    two_float = hidden_two.astype(jnp.float32)
    cot_middle = (conv_block(wrap_all(cot_last), flip_kernel(w_last)) * (1.0 - two_float * two_float)).astype(jnp.bfloat16)
    grad_middle = kernel_grad(wrap_all(hidden_one), cot_middle)
    bias_middle = lax.optimization_barrier(jnp.sum(cot_middle.astype(jnp.float32), axis=(0, 1, 3, 4)))
    one_float = hidden_one.astype(jnp.float32)
    cot_first = (conv_block(wrap_all(cot_middle), flip_kernel(w_middle)) * (1.0 - one_float * one_float)).astype(jnp.bfloat16)
    grad_first = kernel_grad(wrap_all(inputs), cot_first)
    bias_first = lax.optimization_barrier(jnp.sum(cot_first.astype(jnp.float32), axis=(0, 1, 3, 4)))
    d_inputs = conv_block(wrap_all(cot_first), flip_kernel(w_first))
    noise_grad = frozen * d_inputs[:, :, 0] + force_field * (frozen + active * growth) - noise
    return (field, noise_grad, summed / sites, grad_first / sites, bias_first / sites, grad_middle / sites, bias_middle / sites, grad_last / sites, bias_last / sites)
```

```python
import functools

import jax
import jax.numpy as jnp
import numpy as np
from jax import lax
from jax.experimental import pallas as pl
from jax.experimental.pallas import tpu as pltpu
from jax.sharding import PartitionSpec as P

HOPPING = 0.15
QUARTIC = 0.1
F32 = jnp.float32
BF16 = jnp.bfloat16

HALO = 6
ROWS = 2 + 2 * HALO
XP = 10
PACK_ROWS = 344


def tap_selector():
    table = np.zeros((32, 16, 64), np.float32)
    for x in range(2):
        for y in range(2):
            for t in range(4):
                for a in range(3):
                    for b in range(3):
                        for c in range(3):
                            column = (x + a) * 16 + (y + b) * 4 + (t + c - 1) % 4
                            table[a * 9 + b * 3 + c, (x * 2 + y) * 4 + t, column] = 1.0
    return table.reshape(32, 1024)


def roll_z(v, shift):
    shift = shift % 128
    if shift == 0:
        return v
    last = v.ndim - 1
    return jnp.concatenate(
        [pltpu.roll(v[..., :128], shift, last), pltpu.roll(v[..., 128:], shift, last)], axis=last
    )


def swap_halves(v):
    return jnp.concatenate([v[..., 128:], v[..., :128]], axis=v.ndim - 1)


def iota(shape, dim):
    return lax.broadcasted_iota(jnp.int32, shape, dim)


def band_tile(taps, first, rows):
    zero = jnp.zeros((rows, 128), F32)
    left = taps[first] if 0 <= first <= 2 else zero
    right = taps[first + 1] if 0 <= first + 1 <= 2 else zero
    return jnp.where(iota((rows, 128), 1) < 64, left, right)


def build_hidden_band(taps_ref, band_ref):
    zero = jnp.zeros((16, 128), BF16)
    for d in range(3):
        for t in range(4):
            for a in range(3):
                taps = []
                for b in range(3):
                    tap = taps_ref[d * 9 + a * 3 + b].astype(F32)
                    taps.append(pltpu.roll(tap, (16 * (t - 1)) % 128, 1))
                for y in range(2):
                    for pair in range(2):
                        tile = band_tile(taps, 2 * pair - y, 16).astype(BF16)
                        for x in range(2):
                            row = d * 256 + ((x * 2 + y) * 4 + t) * 16
                            lane = ((x + a) * 2 + pair) * 128
                            band_ref[row : row + 16, lane : lane + 128] = tile
            for y in range(2):
                for pair in range(2):
                    for x, far in ((0, 3), (1, 0)):
                        row = d * 256 + ((x * 2 + y) * 4 + t) * 16
                        lane = (far * 2 + pair) * 128
                        band_ref[row : row + 16, lane : lane + 128] = zero


def build_head_band(taps_ref, band_ref):
    for d in range(3):
        for x in range(2):
            for window in range(4):
                a = window - x
                for pair in range(3):
                    for half in range(2):
                        row = d * 64 + x * 32 + half * 16
                        lane = (window * 3 + pair) * 128
                        if 0 <= a <= 2:
                            taps = [taps_ref[d * 9 + a * 3 + b].astype(F32) for b in range(3)]
                            tile = jnp.concatenate(
                                [band_tile(taps, 2 * pair - 2 * half - y, 8) for y in range(2)], axis=0
                            )
                        else:
                            tile = jnp.zeros((16, 128), F32)
                        band_ref[row : row + 16, lane : lane + 128] = tile.astype(BF16)


def combine_z(parts, rows):
    return (
        roll_z(parts[:rows], 1) + parts[rows : 2 * rows] + roll_z(parts[2 * rows :], -1)
    )


def rotate_groups(v, step, lanes):
    if step == 0:
        return v
    group = (iota(v.shape, 1) // lanes) % 4
    ahead = pltpu.roll(v, (128 - lanes * step) % 128, 1)
    behind = pltpu.roll(v, lanes * (4 - step), 1)
    return jnp.where(group + step < 4, ahead, behind)


def rotate_rows(v, step):
    if step == 0:
        return v
    ahead = pltpu.roll(v, v.shape[0] - step, 0)
    behind = pltpu.roll(v, 4 - step, 0)
    return jnp.where(iota(v.shape, 0) % 4 + step < 4, ahead, behind)


def main_kernel(
    place_ref,
    noise_ref,
    small_ref,
    selector_ref,
    taps2_ref,
    taps2t_ref,
    taps3_ref,
    b1_ref,
    b2_ref,
    b3_ref,
    field_out,
    rest_out,
    window_out,
    pack_out,
    nz,
    inp,
    h1,
    h2,
    cm,
    cmr,
    cf,
    cl,
    head,
    phi,
    own_field,
    own_rest,
    w1,
    wl,
    w2,
    w2t,
    w3,
    gm,
    gl,
    gf,
):
    spread = jnp.dot(small_ref[...], selector_ref[...], preferred_element_type=F32)
    for g in range(16):
        piece = spread[:, g * 64 : (g + 1) * 64]
        w1[g * 16 : (g + 1) * 16, :] = jnp.concatenate(
            [piece[16 * k : 16 * k + 16] for k in range(3)], axis=1
        ).astype(BF16)
        wl[g * 16 : (g + 1) * 16, :] = jnp.concatenate(
            [piece[48 + 16 * k : 64 + 16 * k] for k in range(6)], axis=1
        ).astype(BF16)
    build_hidden_band(taps2_ref, w2)
    build_hidden_band(taps2t_ref, w2t)
    build_head_band(taps3_ref, w3)

    rows_in = 4 * ROWS
    shape = (rows_in, 256)
    site = iota(shape, 0) // 4 + iota(shape, 0) % 4 + iota(shape, 1) % 128
    even = site % 2
    for xl in range(8):
        v = jnp.concatenate([noise_ref[xl], noise_ref[xl + 8]], axis=1)
        nz[xl + 1] = v
        if xl == 7:
            nz[0] = swap_halves(v)
        if xl == 0:
            nz[9] = swap_halves(v)
    for xl in range(XP):
        v = jnp.where(even == (xl + 1) % 2, nz[xl], 0.0)
        inp[0, xl] = roll_z(v, 1)
        inp[1, xl] = v
        inp[2, xl] = roll_z(v, -1)

    def wrap(ref):
        ref[0] = swap_halves(ref[8])
        ref[9] = swap_halves(ref[1])

    def first_body(step, _):
        xp = step // 6
        yp = step % 6
        window = inp[:, pl.ds(2 * xp, 4), pl.ds(pl.multiple_of(8 * yp, 8), 16), :]
        window = window.reshape(192, 256).astype(BF16)
        out = jnp.dot(w1[...], window, preferred_element_type=F32)
        out = jnp.tanh(out.reshape(16, 16, 256) + b1_ref[...][None]).reshape(256, 256).astype(BF16)
        row = pl.ds(pl.multiple_of(yp * 128, 128), 128)
        h1[2 * xp + 1, row, :] = out[:128]
        h1[2 * xp + 2, row, :] = out[128:]
        return 0

    lax.fori_loop(0, 24, first_body, 0)
    wrap(h1)

    def second_body(step, _):
        xp = step // 5
        yp = step % 5
        window = h1[pl.ds(2 * xp, 4), pl.ds(pl.multiple_of(yp * 128, 128), 256), :].reshape(1024, 256)
        parts = jnp.dot(w2[...], window, preferred_element_type=F32)
        out = combine_z(parts, 256)
        out = jnp.tanh(out.reshape(16, 16, 256) + b2_ref[...][None]).reshape(256, 256).astype(BF16)
        row = pl.ds(pl.multiple_of(yp * 128, 128), 128)
        h2[2 * xp + 1, row, :] = out[:128]
        h2[2 * xp + 2, row, :] = out[128:]
        return 0

    lax.fori_loop(0, 20, second_body, 0)
    wrap(h2)

    top = iota((8, 256), 0) < 4

    def head_body(step, _):
        xp = step // 2
        yq = step % 2
        window = h2[pl.ds(2 * xp, 4), pl.ds(pl.multiple_of(yq * 256, 256), 384), :].reshape(1536, 256)
        parts = jnp.dot(w3[...], window, preferred_element_type=F32)
        out = combine_z(parts, 64)
        out = (out.reshape(8, 8, 256) + b3_ref[...][None]).reshape(64, 256)
        for x in range(2):
            for pair in range(2):
                base = x * 32 + pair * 16
                lower = out[base : base + 8]
                upper = out[base + 8 : base + 16]
                row = pl.ds(pl.multiple_of(yq * 16, 16) + pair * 8, 8)
                head[0, 2 * xp + x, row, :] = jnp.where(top, lower, pltpu.roll(upper, 4, 0))
                head[1, 2 * xp + x, row, :] = jnp.where(top, pltpu.roll(lower, 4, 0), upper)
        return 0

    lax.fori_loop(0, 8, head_body, 0)

    shape = (32, 256)
    row32 = iota(shape, 0)
    site = row32 // 4 + 1 + row32 % 4 + iota(shape, 1) % 128
    even = site % 2
    for xl in range(8):
        frozen = even == xl % 2
        noise = nz[xl + 1, 12:44, :]
        log_scale = jnp.tanh(head[0, xl])
        head[0, xl] = log_scale
        moved = noise * jnp.exp(log_scale) + head[1, xl]
        phi[xl + 1] = jnp.where(frozen, noise, moved)
    wrap(phi)

    own = (row32 >= 12) & (row32 < 20)
    inner_t = row32 % 4
    loss = jnp.zeros(shape, F32)
    cot_sum = [jnp.zeros((8, 256), F32), jnp.zeros((8, 256), F32)]
    for xl in range(8):
        frozen = even == xl % 2
        noise = nz[xl + 1, 12:44, :]
        log_scale = head[0, xl]
        growth = jnp.exp(log_scale)
        here = phi[xl + 1]
        upward = (
            phi[xl + 2]
            + pltpu.roll(here, 28, 0)
            + jnp.where(inner_t == 3, pltpu.roll(here, 3, 0), pltpu.roll(here, 31, 0))
            + roll_z(here, -1)
        )
        downward = (
            phi[xl]
            + pltpu.roll(here, 4, 0)
            + jnp.where(inner_t == 0, pltpu.roll(here, 29, 0), pltpu.roll(here, 1, 0))
            + roll_z(here, 1)
        )
        squared = here * here
        density = (
            -2.0 * HOPPING * here * upward + squared + QUARTIC * (squared - 1.0) * (squared - 1.0)
        )
        local = -0.5 * noise * noise - jnp.where(frozen, 0.0, log_scale) + density
        loss = loss + jnp.where(own, local, 0.0)
        force = (
            -2.0 * HOPPING * (upward + downward)
            + 2.0 * here
            + 4.0 * QUARTIC * here * (squared - 1.0)
        )
        d_scale = (force * noise * growth - 1.0) * (1.0 - log_scale * log_scale)
        pair = (jnp.where(frozen, 0.0, d_scale), jnp.where(frozen, 0.0, force))
        rest = force * jnp.where(frozen, 1.0, growth) - noise
        own_field[xl] = here[12:20]
        own_rest[xl] = rest[12:20]
        for ch in range(2):
            v = pltpu.roll(pair[ch], 28, 0)[:24].astype(BF16).astype(F32)
            cot_sum[ch] = cot_sum[ch] + v[8:16]
            for d, shift in ((0, 1), (1, 0), (2, -1)):
                moved = roll_z(v, shift)
                cl[d, ch, xl + 1] = moved
                if xl == 7:
                    cl[d, ch, 0] = swap_halves(moved)
                if xl == 0:
                    cl[d, ch, 9] = swap_halves(moved)

    def middle_body(step, _):
        xp = step // 2
        yp = step % 2
        window = cl[:, :, pl.ds(2 * xp, 4), pl.ds(pl.multiple_of(8 * yp, 8), 16), :]
        window = window.reshape(384, 256).astype(BF16)
        out = jnp.dot(wl[...], window, preferred_element_type=F32)
        for x in range(2):
            hidden = h2[2 * xp + 1 + x, pl.ds(pl.multiple_of((3 + 2 * yp) * 64, 64), 128), :].astype(F32)
            v = out[128 * x : 128 * x + 128] * (1.0 - hidden * hidden)
            cm[2 * xp + 1 + x, pl.ds(pl.multiple_of(yp * 128, 128), 128), :] = v.astype(BF16)
        return 0

    lax.fori_loop(0, 8, middle_body, 0)
    wrap(cm)

    def shift_body(xl, _):
        v = cm[xl, 64:192, :].astype(F32)
        cmr[0, xl] = roll_z(v, -1).astype(BF16)
        cmr[1, xl] = v.astype(BF16)
        cmr[2, xl] = roll_z(v, 1).astype(BF16)
        return 0

    lax.fori_loop(0, XP, shift_body, 0)

    def first_cot_body(xp, _):
        window = cm[pl.ds(2 * xp, 4)].reshape(1024, 256)
        parts = jnp.dot(w2t[...], window, preferred_element_type=F32)
        out = combine_z(parts, 256)
        for x in range(2):
            hidden = h1[2 * xp + 1 + x, 320:448, :].astype(F32)
            v = out[128 * x : 128 * x + 128] * (1.0 - hidden * hidden)
            cf[2 * xp + 1 + x] = v.astype(BF16)
        return 0

    lax.fori_loop(0, 4, first_cot_body, 0)
    wrap(cf)

    gm[...] = jnp.zeros_like(gm)
    gl[...] = jnp.zeros_like(gl)
    gf[...] = jnp.zeros_like(gf)
    over_lanes = (((1,), (1,)), ((), ()))

    def grad_body(xl, _):
        left = cmr[:, pl.ds(xl - 1, 3)].reshape(1152, 256)
        gm[...] += lax.dot_general(left, h1[xl, 256:512, :], over_lanes, preferred_element_type=F32)
        left = cl[:, :, pl.ds(xl - 1, 3), 8:16, :].reshape(144, 256).astype(BF16)
        gl[...] += lax.dot_general(left, h2[xl, 192:448, :], over_lanes, preferred_element_type=F32)
        left = inp[:, pl.ds(xl - 1, 3), 20:36, :].reshape(144, 256).astype(BF16)
        gf[...] += lax.dot_general(left, cf[xl], over_lanes, preferred_element_type=F32)
        return 0

    lax.fori_loop(1, 9, grad_body, 0)

    low = iota((16, 128), 1) < 64
    third = []
    for g in range(9):
        sums = []
        for y in range(2):
            for side in range(2):
                total = None
                for t in range(4):
                    row = g * 128 + y * 64 + t * 16
                    block = gm[row : row + 16, side * 128 : side * 128 + 128]
                    block = rotate_groups(block, (t - 1) % 4, 16)
                    total = block if total is None else total + block
                sums.append(total)
        u0, u1, v0, v1 = sums
        v0 = pltpu.roll(v0, 64, 1)
        v1 = pltpu.roll(v1, 64, 1)
        pack_out[g * 16 : g * 16 + 16, :] = u0 + jnp.where(low, v0, v1)
        third.append(u1 + v1)
    third.append(third[8])
    for g in range(5):
        packed = jnp.where(low, third[2 * g], pltpu.roll(third[2 * g + 1], 64, 1))
        pack_out[144 + g * 16 : 160 + g * 16, :] = packed

    shape = (144, 128)
    row144 = iota(shape, 0)
    sides = []
    for side in range(2):
        v = gl[:, side * 128 : side * 128 + 128]
        total = jnp.zeros(shape, F32)
        for t in range(4):
            total = total + jnp.where(row144 % 4 == t, rotate_groups(v, (t - 1) % 4, 16), 0.0)
        sides.append(total)
    lower_y = (row144 // 4) % 2 == 0
    r0, r1 = sides
    s0 = pltpu.roll(r0, 64, 1)
    s1 = pltpu.roll(r1, 64, 1)
    low = iota(shape, 1) < 64
    both = jnp.where(lower_y, r0, jnp.where(low, s0, s1))
    last = jnp.where(lower_y, r1, s1)
    pack_out[256:304, :] = jnp.zeros((48, 128), F32)
    pack_out[256:274, :] = both.reshape(18, 8, 128).sum(axis=1)
    pack_out[280:298, :] = last.reshape(18, 8, 128).sum(axis=1)

    v = gf[...]
    total = jnp.zeros(shape, F32)
    for y in range(2):
        for t in range(4):
            moved = v if y + t == 0 else pltpu.roll(v, 128 - (y * 64 + t * 16), 1)
            if y:
                moved = pltpu.roll(moved, 140, 0)
            total = total + rotate_rows(moved, (t - 1) % 4)
    total = jnp.where(iota(shape, 1) < 16, total, 0.0)
    packed = total[:16]
    for g in range(1, 8):
        packed = packed + pltpu.roll(total[g * 16 : g * 16 + 16], 16 * g, 1)
    pack_out[224:240, :] = packed
    pack_out[240:256, :] = total[128:144]

    def channel_sum(read, base):
        acc = None
        for xl in range(1, 9):
            v = read(xl).astype(F32)
            v = v[:, :128] + v[:, 128:]
            acc = v if acc is None else acc + v
        acc = acc.reshape(8, 16, 128).sum(axis=0)
        pack_out[base : base + 16, :] = jnp.broadcast_to(jnp.sum(acc, axis=1, keepdims=True), (16, 128))

    channel_sum(lambda xl: cm[xl, 64:192, :], 304)
    channel_sum(lambda xl: cf[xl], 320)
    row8 = iota((8, 128), 0)
    tile = jnp.where(row8 == 0, jnp.sum(cot_sum[0]), 0.0)
    tile = jnp.where(row8 == 1, jnp.sum(cot_sum[1]), tile)
    pack_out[336:344, :] = jnp.where(row8 == 2, jnp.sum(loss), tile)

    place = place_ref[0]
    start = 2 * (place % 4)
    high = place >= 4

    def pick(v):
        return jnp.where(high, v[:, 128:], v[:, :128])

    for x in range(2):
        field_out[x] = pick(own_field[start + x])
        rest_out[x] = pick(own_rest[start + x])
    for x in range(4):
        window_out[x] = pick(cf[start + x])


def input_kernel(left_ref, own_ref, right_ref, taps_ref, rest_ref, out_ref, band):
    shape = (8, 128)
    upper = iota(shape, 0) < 4
    zero = jnp.zeros(shape, F32)
    for d in range(3):
        for window in range(4):
            for pair in range(2):
                tiles = []
                for x in range(2):
                    a = window - x
                    if 0 <= a <= 2:
                        taps = [taps_ref[d * 9 + a * 3 + b].astype(F32) for b in range(3)]
                        tiles.append(
                            jnp.where(
                                upper, band_tile(taps, 2 * pair, 8), band_tile(taps, 2 * pair - 1, 8)
                            )
                        )
                    else:
                        tiles.append(zero)
                lane = (window * 2 + pair) * 128
                band[d * 16 : d * 16 + 16, lane : lane + 128] = jnp.concatenate(tiles, axis=0).astype(BF16)
    window = jnp.concatenate([left_ref[...], own_ref[...], right_ref[...]], axis=1).reshape(1024, 128)
    parts = jnp.dot(band[...], window, preferred_element_type=F32)
    out = pltpu.roll(parts[:16], 1, 1) + parts[16:32] + pltpu.roll(parts[32:], 127, 1)
    site = iota(shape, 0) // 4 + iota(shape, 0) % 4 + iota(shape, 1)
    for x in range(2):
        out_ref[x] = jnp.where((site + x) % 2 == 0, out[8 * x : 8 * x + 8], 0.0) + rest_ref[x]


def vmem():
    return pl.BlockSpec(memory_space=pltpu.VMEM)


def run_main(place, noise, small, selector, taps2, taps2t, taps3, b1, b2, b3):
    scratch = [
        ((XP, 4 * ROWS, 256), F32),
        ((3, XP, 4 * ROWS, 256), F32),
        ((XP, 768, 256), BF16),
        ((XP, 640, 256), BF16),
        ((XP, 256, 256), BF16),
        ((3, XP, 128, 256), BF16),
        ((XP, 128, 256), BF16),
        ((3, 2, XP, 24, 256), F32),
        ((2, 8, 32, 256), F32),
        ((XP, 32, 256), F32),
        ((8, 8, 256), F32),
        ((8, 8, 256), F32),
        ((256, 192), BF16),
        ((256, 384), BF16),
        ((768, 1024), BF16),
        ((768, 1024), BF16),
        ((192, 1536), BF16),
        ((1152, 256), F32),
        ((144, 256), F32),
        ((144, 128), F32),
    ]
    return pl.pallas_call(
        main_kernel,
        out_shape=(
            jax.ShapeDtypeStruct((2, 8, 128), F32),
            jax.ShapeDtypeStruct((2, 8, 128), F32),
            jax.ShapeDtypeStruct((4, 128, 128), BF16),
            jax.ShapeDtypeStruct((PACK_ROWS, 128), F32),
        ),
        in_specs=[pl.BlockSpec(memory_space=pltpu.SMEM)] + [vmem()] * 9,
        out_specs=(vmem(), vmem(), vmem(), vmem()),
        scratch_shapes=[pltpu.VMEM(s, t) for s, t in scratch],
        compiler_params=pltpu.CompilerParams(vmem_limit_bytes=56 * 1024 * 1024),
    )(place, noise, small, selector, taps2, taps2t, taps3, b1, b2, b3)


def run_input(left, own, right, taps, rest):
    return pl.pallas_call(
        input_kernel,
        out_shape=jax.ShapeDtypeStruct((2, 8, 128), F32),
        in_specs=[vmem()] * 5,
        out_specs=vmem(),
        scratch_shapes=[pltpu.VMEM((48, 1024), BF16)],
        compiler_params=pltpu.CompilerParams(vmem_limit_bytes=16 * 1024 * 1024),
    )(left, own, right, taps, rest)


def pad_taps(v):
    return jnp.pad(v, [(0, 0)] * (v.ndim - 2) + [(0, 1), (0, 0)])


def hidden_taps(kernel):
    v = pad_taps(jnp.transpose(kernel, (5, 2, 3, 0, 4, 1))).reshape(27, 16, 64)
    return jnp.concatenate([v, v], axis=2)


def banded_taps(v):
    v = pad_taps(v)
    v = jnp.stack([jnp.roll(v, t - 1, axis=2) for t in range(4)], axis=2)
    v = v.reshape(27, -1, 64)
    return jnp.concatenate([v, v], axis=2)


def swapped(v, axis_size, partner):
    return lax.ppermute(v, "gy", [(i, partner(i)) for i in range(axis_size)])


def gather_noise(noise):
    size_y = lax.axis_size("gy")
    size_x = lax.axis_size("gx")
    even = lax.axis_index("gy") % 2 == 0
    chips = size_y // 2

    def far(i):
        return (i - 3) % size_y if i % 2 == 0 else (i + 3) % size_y

    def chip_after(i):
        return ((((i >> 1) + 1) ^ 1) - 1) % chips * 2 + (i & 1)

    distant = swapped(noise, size_y, far)
    beside = swapped(noise, size_y, lambda i: i ^ 1)
    block = jnp.concatenate(
        [jnp.where(even, noise, beside), jnp.where(even, beside, noise)], axis=1
    )
    paired = swapped(block, size_y, lambda i: i ^ 2)
    across = swapped(block, size_y, chip_after)
    even_chip = (lax.axis_index("gy") // 2) % 2 == 0
    before = jnp.where(even_chip, across, paired)
    after = jnp.where(even_chip, paired, across)
    middle = jnp.concatenate([before, block, after], axis=1)
    window = jnp.where(
        even,
        jnp.concatenate([distant, middle], axis=1),
        jnp.concatenate([middle, distant], axis=1),
    )
    window = window.reshape(2, 4 * ROWS, 128)
    sent = jnp.broadcast_to(window[None], (size_x,) + window.shape)
    return lax.all_to_all(sent, "gx", 0, 0, tiled=True).reshape(16, 4 * ROWS, 128)


def sum_over_y(v):
    size_y = lax.axis_size("gy")

    def along_z(partner):
        def f(i):
            return ((i >> 4) * 8 + partner((i >> 1) & 7)) * 2 + (i & 1)

        return f

    crossing = (3, 6, 5, 0, 7, 2, 1, 4)
    for partner in (
        lambda i: i ^ 1,
        lambda i: i ^ 16,
        along_z(lambda z: z ^ 1),
        along_z(lambda z: (((z + 1) ^ 1) - 1) % 8),
        along_z(lambda z: crossing[z]),
    ):
        v = v + swapped(v, size_y, partner)
    return v


def local(noise, w_first, b_first, w_middle, b_middle, w_last, b_last):
    size_y = lax.axis_size("gy")
    sites = float(noise.size * lax.axis_size("gx") * size_y)
    flip = (slice(None), slice(None)) + (slice(None, None, -1),) * 4
    small = jnp.concatenate(
        [
            jnp.transpose(w_first[:, 0], (4, 0, 1, 2, 3)).reshape(48, 27),
            jnp.transpose(w_last[flip], (5, 0, 1, 2, 3, 4)).reshape(96, 27),
        ],
        axis=0,
    )
    small = jnp.pad(small, ((0, 0), (0, 5)))
    taps2 = hidden_taps(w_middle)
    taps2t = hidden_taps(jnp.transpose(w_middle[flip], (1, 0, 2, 3, 4, 5)))
    taps3 = banded_taps(jnp.transpose(w_last, (5, 2, 3, 0, 4, 1)).reshape(27, 2, 3, 16))
    tapsd = banded_taps(jnp.transpose(w_first[flip], (5, 2, 3, 1, 4, 0)).reshape(27, 1, 3, 16))
    tapsd = jnp.concatenate([tapsd, tapsd], axis=1)

    gathered = gather_noise(noise)
    place = lax.axis_index("gx").astype(jnp.int32).reshape(1)
    field, rest, window, pack = run_main(
        place,
        gathered,
        small,
        jnp.asarray(tap_selector(), BF16),
        taps2,
        taps2t,
        taps3,
        b_first.reshape(16, 1),
        b_middle.reshape(16, 1),
        jnp.repeat(b_last, 4).reshape(8, 1),
    )
    left = swapped(window[:, 64:], size_y, lambda i: (i + 1) % size_y)
    right = swapped(window[:, :64], size_y, lambda i: (i - 1) % size_y)
    noise_grad = run_input(left, window, right, tapsd, rest)

    total = sum_over_y(pack) * (1.0 / sites)
    most = total[:144].reshape(3, 3, 16, 2, 4, 16)
    third = total[144:224].reshape(5, 16, 2, 4, 16)
    third = jnp.transpose(third, (0, 2, 1, 3, 4)).reshape(10, 16, 4, 16)[:9].reshape(3, 3, 16, 1, 4, 16)
    middle = jnp.concatenate([most, third], axis=3)[:, ::-1, :, :, :3]
    grad_middle = jnp.transpose(middle, (2, 5, 1, 3, 4, 0))
    first = jnp.concatenate([total[224:240], total[240:256, :16]], axis=1).reshape(4, 4, 3, 3, 16)
    grad_first = jnp.transpose(first[:3, :3], (4, 3, 0, 1, 2))[:, None]
    last = jnp.concatenate([total[256:274], total[280:298, :64]], axis=1)
    last = last.reshape(3, 2, 3, 3, 4, 16)[::-1, :, ::-1, :, :3]
    grad_last = jnp.transpose(last, (1, 5, 2, 3, 4, 0))
    return (
        field.reshape(noise.shape),
        noise_grad.reshape(noise.shape),
        total[338, 0],
        grad_first,
        total[320:336, 0],
        grad_middle,
        total[304:320, 0],
        grad_last,
        total[336:338, 0],
    )


def solution(mesh):
    placed = (P("gx", "gy", None, None), P(), P(), P(), P(), P(), P())
    return jax.shard_map(
        local,
        mesh=mesh,
        in_specs=placed,
        out_specs=(P("gx", "gy", None, None), P("gx", "gy", None, None)) + (P(),) * 7,
        check_vma=False,
    )
```

```python
import functools

import jax
import jax.numpy as jnp
import numpy as np
from jax import lax
from jax.experimental import pallas as pl
from jax.experimental.pallas import tpu as pltpu
from jax.sharding import PartitionSpec as P

HOPPING = 0.15
QUARTIC = 0.1
F32 = jnp.float32
BF16 = jnp.bfloat16

HALO = 6
ROWS = 2 + 2 * HALO
XP = 10
PACK_ROWS = 288
GROUP = 8


def tap_selector():
    table = np.zeros((32, 16, 64), np.float32)
    for x in range(2):
        for y in range(2):
            for t in range(4):
                for a in range(3):
                    for b in range(3):
                        for c in range(3):
                            column = (x + a) * 16 + (y + b) * 4 + (t + c - 1) % 4
                            table[a * 9 + b * 3 + c, (x * 2 + y) * 4 + t, column] = 1.0
    return table.reshape(32, 1024)


def roll_z(v, shift):
    shift = shift % 128
    if shift == 0:
        return v
    last = v.ndim - 1
    return jnp.concatenate(
        [pltpu.roll(v[..., :128], shift, last), pltpu.roll(v[..., 128:], shift, last)], axis=last
    )


def swap_halves(v):
    return jnp.concatenate([v[..., 128:], v[..., :128]], axis=v.ndim - 1)


def iota(shape, dim):
    return lax.broadcasted_iota(jnp.int32, shape, dim)


def band_tile(taps, first, rows):
    zero = jnp.zeros((rows, 128), F32)
    left = taps[first] if 0 <= first <= 2 else zero
    right = taps[first + 1] if 0 <= first + 1 <= 2 else zero
    return jnp.where(iota((rows, 128), 1) < 64, left, right)


def build_hidden_band(taps_ref, band_ref):
    for d in range(3):
        for t in range(4):
            for a in range(3):
                taps = []
                for b in range(3):
                    tap = taps_ref[d * 9 + a * 3 + b].astype(F32)
                    taps.append(pltpu.roll(tap, (16 * (t - 1)) % 128, 1))
                for y in range(2):
                    for pair in range(2):
                        row = d * 128 + (y * 4 + t) * 16
                        lane = (a * 2 + pair) * 128
                        tile = band_tile(taps, 2 * pair - y, 16)
                        band_ref[row : row + 16, lane : lane + 128] = tile.astype(BF16)


def build_head_band(taps_ref, band_ref):
    for d in range(3):
        for x in range(2):
            for window in range(4):
                a = window - x
                for pair in range(3):
                    for half in range(2):
                        row = d * 64 + x * 32 + half * 16
                        lane = (window * 3 + pair) * 128
                        if 0 <= a <= 2:
                            taps = [taps_ref[d * 9 + a * 3 + b].astype(F32) for b in range(3)]
                            tile = jnp.concatenate(
                                [band_tile(taps, 2 * pair - 2 * half - y, 8) for y in range(2)], axis=0
                            )
                        else:
                            tile = jnp.zeros((16, 128), F32)
                        band_ref[row : row + 16, lane : lane + 128] = tile.astype(BF16)


def combine_z(parts, rows):
    return (
        roll_z(parts[:rows], 1) + parts[rows : 2 * rows] + roll_z(parts[2 * rows :], -1)
    )


def rotate_groups(v, step, lanes):
    if step == 0:
        return v
    group = (iota(v.shape, 1) // lanes) % 4
    ahead = pltpu.roll(v, (128 - lanes * step) % 128, 1)
    behind = pltpu.roll(v, lanes * (4 - step), 1)
    return jnp.where(group + step < 4, ahead, behind)


def rotate_rows(v, step):
    if step == 0:
        return v
    ahead = pltpu.roll(v, v.shape[0] - step, 0)
    behind = pltpu.roll(v, 4 - step, 0)
    return jnp.where(iota(v.shape, 0) % 4 + step < 4, ahead, behind)


def main_kernel(
    place_ref,
    noise_ref,
    small_ref,
    selector_ref,
    taps2_ref,
    taps2t_ref,
    taps3_ref,
    b1_ref,
    b2_ref,
    b3_ref,
    field_out,
    rest_out,
    window_out,
    partner_out,
    beyond_out,
    mine_out,
    theirs_out,
    nz,
    inp,
    h1,
    h2,
    cm,
    cmr,
    cf,
    cl,
    head,
    phi,
    own_field,
    own_rest,
    w1,
    wl,
    w2,
    w2t,
    w3,
    gm,
    gl,
    gf,
    pack_out,
):
    spread = jnp.dot(small_ref[...], selector_ref[...], preferred_element_type=F32)
    for g in range(16):
        piece = spread[:, g * 64 : (g + 1) * 64]
        w1[g * 16 : (g + 1) * 16, :] = jnp.concatenate(
            [piece[16 * k : 16 * k + 16] for k in range(3)], axis=1
        ).astype(BF16)
        wl[g * 16 : (g + 1) * 16, :] = jnp.concatenate(
            [piece[48 + 16 * k : 64 + 16 * k] for k in range(6)], axis=1
        ).astype(BF16)
    build_hidden_band(taps2_ref, w2)
    build_hidden_band(taps2t_ref, w2t)
    build_head_band(taps3_ref, w3)

    rows_in = 4 * ROWS
    shape = (rows_in, 256)
    site = iota(shape, 0) // 4 + iota(shape, 0) % 4 + iota(shape, 1) % 128
    even = site % 2
    for xl in range(8):
        v = jnp.concatenate([noise_ref[xl], noise_ref[xl + 8]], axis=1)
        nz[xl + 1] = v
        if xl == 7:
            nz[0] = swap_halves(v)
        if xl == 0:
            nz[9] = swap_halves(v)
    for xl in range(XP):
        v = jnp.where(even == (xl + 1) % 2, nz[xl], 0.0)
        inp[0, xl] = roll_z(v, 1)
        inp[1, xl] = v
        inp[2, xl] = roll_z(v, -1)

    def wrap(ref):
        ref[0] = swap_halves(ref[8])
        ref[9] = swap_halves(ref[1])

    def first_body(step, _):
        xp = step // 6
        yp = step % 6
        window = inp[:, pl.ds(2 * xp, 4), pl.ds(pl.multiple_of(8 * yp, 8), 16), :]
        window = window.reshape(192, 256).astype(BF16)
        out = jnp.dot(w1[...], window, preferred_element_type=F32)
        out = jnp.tanh(out.reshape(16, 16, 256) + b1_ref[...][None]).reshape(256, 256).astype(BF16)
        row = pl.ds(pl.multiple_of(yp * 128, 128), 128)
        h1[2 * xp + 1, row, :] = out[:128]
        h1[2 * xp + 2, row, :] = out[128:]
        return 0

    lax.fori_loop(0, 24, first_body, 0, unroll=12)
    wrap(h1)

    def second_body(step, _):
        xl = step // 5
        yp = step % 5
        window = h1[pl.ds(xl, 3), pl.ds(pl.multiple_of(yp * 128, 128), 256), :].reshape(768, 256)
        parts = jnp.dot(w2[...], window, preferred_element_type=F32)
        out = combine_z(parts, 128)
        out = jnp.tanh(out.reshape(8, 16, 256) + b2_ref[...][None]).reshape(128, 256)
        h2[xl + 1, pl.ds(pl.multiple_of(yp * 128, 128), 128), :] = out.astype(BF16)
        return 0

    lax.fori_loop(0, 40, second_body, 0, unroll=20)
    wrap(h2)

    top = iota((8, 256), 0) < 4

    def head_body(step, _):
        xp = step // 2
        yq = step % 2
        window = h2[pl.ds(2 * xp, 4), pl.ds(pl.multiple_of(yq * 256, 256), 384), :].reshape(1536, 256)
        parts = jnp.dot(w3[...], window, preferred_element_type=F32)
        out = combine_z(parts, 64)
        out = (out.reshape(8, 8, 256) + b3_ref[...][None]).reshape(64, 256)
        for x in range(2):
            for pair in range(2):
                base = x * 32 + pair * 16
                lower = out[base : base + 8]
                upper = out[base + 8 : base + 16]
                row = pl.ds(pl.multiple_of(yq * 16, 16) + pair * 8, 8)
                head[0, 2 * xp + x, row, :] = jnp.where(top, lower, pltpu.roll(upper, 4, 0))
                head[1, 2 * xp + x, row, :] = jnp.where(top, pltpu.roll(lower, 4, 0), upper)
        return 0

    lax.fori_loop(0, 8, head_body, 0, unroll=8)

    shape = (32, 256)
    row32 = iota(shape, 0)
    site = row32 // 4 + 1 + row32 % 4 + iota(shape, 1) % 128
    even = site % 2
    for xl in range(8):
        frozen = even == xl % 2
        noise = nz[xl + 1, 12:44, :]
        log_scale = jnp.tanh(head[0, xl])
        head[0, xl] = log_scale
        moved = noise * jnp.exp(log_scale) + head[1, xl]
        phi[xl + 1] = jnp.where(frozen, noise, moved)
    wrap(phi)

    own = (row32 >= 12) & (row32 < 20)
    inner_t = row32 % 4
    loss = jnp.zeros(shape, F32)
    cot_sum = [jnp.zeros((8, 256), F32), jnp.zeros((8, 256), F32)]
    for xl in range(8):
        frozen = even == xl % 2
        noise = nz[xl + 1, 12:44, :]
        log_scale = head[0, xl]
        growth = jnp.exp(log_scale)
        here = phi[xl + 1]
        upward = (
            phi[xl + 2]
            + pltpu.roll(here, 28, 0)
            + jnp.where(inner_t == 3, pltpu.roll(here, 3, 0), pltpu.roll(here, 31, 0))
            + roll_z(here, -1)
        )
        downward = (
            phi[xl]
            + pltpu.roll(here, 4, 0)
            + jnp.where(inner_t == 0, pltpu.roll(here, 29, 0), pltpu.roll(here, 1, 0))
            + roll_z(here, 1)
        )
        squared = here * here
        density = (
            -2.0 * HOPPING * here * upward + squared + QUARTIC * (squared - 1.0) * (squared - 1.0)
        )
        local = -0.5 * noise * noise - jnp.where(frozen, 0.0, log_scale) + density
        loss = loss + jnp.where(own, local, 0.0)
        force = (
            -2.0 * HOPPING * (upward + downward)
            + 2.0 * here
            + 4.0 * QUARTIC * here * (squared - 1.0)
        )
        d_scale = (force * noise * growth - 1.0) * (1.0 - log_scale * log_scale)
        pair = (jnp.where(frozen, 0.0, d_scale), jnp.where(frozen, 0.0, force))
        rest = force * jnp.where(frozen, 1.0, growth) - noise
        own_field[xl] = here[12:20]
        own_rest[xl] = rest[12:20]
        for ch in range(2):
            v = pltpu.roll(pair[ch], 28, 0)[:24].astype(BF16).astype(F32)
            cot_sum[ch] = cot_sum[ch] + v[8:16]
            for d, shift in ((0, 1), (1, 0), (2, -1)):
                moved = roll_z(v, shift)
                cl[d, ch, xl + 1] = moved
                if xl == 7:
                    cl[d, ch, 0] = swap_halves(moved)
                if xl == 0:
                    cl[d, ch, 9] = swap_halves(moved)

    def middle_body(step, _):
        xp = step // 2
        yp = step % 2
        window = cl[:, :, pl.ds(2 * xp, 4), pl.ds(pl.multiple_of(8 * yp, 8), 16), :]
        window = window.reshape(384, 256).astype(BF16)
        out = jnp.dot(wl[...], window, preferred_element_type=F32)
        for x in range(2):
            hidden = h2[2 * xp + 1 + x, pl.ds(pl.multiple_of((3 + 2 * yp) * 64, 64), 128), :].astype(F32)
            v = out[128 * x : 128 * x + 128] * (1.0 - hidden * hidden)
            cm[2 * xp + 1 + x, pl.ds(pl.multiple_of(yp * 128, 128), 128), :] = v.astype(BF16)
        return 0

    lax.fori_loop(0, 8, middle_body, 0, unroll=8)
    wrap(cm)

    def shift_body(xl, _):
        v = cm[xl, 64:192, :].astype(F32)
        cmr[0, xl] = roll_z(v, -1).astype(BF16)
        cmr[1, xl] = v.astype(BF16)
        cmr[2, xl] = roll_z(v, 1).astype(BF16)
        return 0

    lax.fori_loop(0, XP, shift_body, 0, unroll=5)

    def first_cot_body(xl, _):
        window = cm[pl.ds(xl, 3)].reshape(768, 256)
        parts = jnp.dot(w2t[...], window, preferred_element_type=F32)
        out = combine_z(parts, 128)
        hidden = h1[xl + 1, 320:448, :].astype(F32)
        cf[xl + 1] = (out * (1.0 - hidden * hidden)).astype(BF16)
        return 0

    lax.fori_loop(0, 8, first_cot_body, 0, unroll=8)
    wrap(cf)

    gm[...] = jnp.zeros_like(gm)
    gl[...] = jnp.zeros_like(gl)
    gf[...] = jnp.zeros_like(gf)
    over_lanes = (((1,), (1,)), ((), ()))

    def grad_body(step, _):
        xs = [GROUP * step + 1 + k for k in range(GROUP)]

        def along(parts):
            return jnp.concatenate(parts, axis=1)

        left = along([cmr[:, pl.ds(x - 1, 3)].reshape(1152, 256) for x in xs])
        right = along([h1[x, 256:512, :] for x in xs])
        gm[...] += lax.dot_general(left, right, over_lanes, preferred_element_type=F32)
        left = along([cl[:, :, pl.ds(x - 1, 3), 8:16, :].reshape(144, 256).astype(BF16) for x in xs])
        right = along([h2[x, 192:448, :] for x in xs])
        gl[...] += lax.dot_general(left, right, over_lanes, preferred_element_type=F32)
        left = along([inp[:, pl.ds(x - 1, 3), 20:36, :].reshape(144, 256).astype(BF16) for x in xs])
        right = along([cf[x] for x in xs])
        gf[...] += lax.dot_general(left, right, over_lanes, preferred_element_type=F32)
        return 0

    lax.fori_loop(0, 8 // GROUP, grad_body, 0)

    low = iota((16, 128), 1) < 64
    third = []
    for g in range(9):
        sums = []
        for y in range(2):
            for side in range(2):
                total = None
                for t in range(4):
                    row = g * 128 + y * 64 + t * 16
                    block = gm[row : row + 16, side * 128 : side * 128 + 128]
                    block = rotate_groups(block, (t - 1) % 4, 16)
                    total = block if total is None else total + block
                sums.append(total)
        u0, u1, v0, v1 = sums
        v0 = pltpu.roll(v0, 64, 1)
        v1 = pltpu.roll(v1, 64, 1)
        pack_out[g * 16 : g * 16 + 16, :] = u0 + jnp.where(low, v0, v1)
        third.append(u1 + v1)
    v = gf[...]
    shape = (144, 128)
    total = jnp.zeros(shape, F32)
    for y in range(2):
        for t in range(4):
            moved = v if y + t == 0 else pltpu.roll(v, 128 - (y * 64 + t * 16), 1)
            if y:
                moved = pltpu.roll(moved, 140, 0)
            total = total + rotate_rows(moved, (t - 1) % 4)
    total = jnp.where(iota(shape, 1) < 16, total, 0.0)
    packed = total[:16]
    for g in range(1, 8):
        packed = packed + pltpu.roll(total[g * 16 : g * 16 + 16], 16 * g, 1)
    pack_out[224:240, :] = packed
    third.append(total[128:144])
    for g in range(5):
        packed = jnp.where(low, third[2 * g], pltpu.roll(third[2 * g + 1], 64, 1))
        pack_out[144 + g * 16 : 160 + g * 16, :] = packed

    shape = (144, 128)
    row144 = iota(shape, 0)
    sides = []
    for side in range(2):
        v = gl[:, side * 128 : side * 128 + 128]
        total = jnp.zeros(shape, F32)
        for t in range(4):
            total = total + jnp.where(row144 % 4 == t, rotate_groups(v, (t - 1) % 4, 16), 0.0)
        sides.append(total)
    lower_y = (row144 // 4) % 2 == 0
    r0, r1 = sides
    s0 = pltpu.roll(r0, 64, 1)
    s1 = pltpu.roll(r1, 64, 1)
    low = iota(shape, 1) < 64
    both = jnp.where(lower_y, r0, jnp.where(low, s0, s1))
    last = jnp.where(lower_y, r1, s1)
    pack_out[240:288, :] = jnp.zeros((48, 128), F32)
    pack_out[240:258, :] = both.reshape(18, 8, 128).sum(axis=1)
    pack_out[264:282, :] = last.reshape(18, 8, 128).sum(axis=1)

    diagonal = iota((16, 128), 0) == iota((16, 128), 1)

    def channel_sum(read):
        acc = None
        for xl in range(1, 9):
            v = read(xl).astype(F32)
            v = v[:, :128] + v[:, 128:]
            acc = v if acc is None else acc + v
        acc = jnp.sum(acc.reshape(8, 16, 128).sum(axis=0), axis=1, keepdims=True)
        return jnp.sum(jnp.where(diagonal, acc, 0.0), axis=0, keepdims=True)

    pack_out[258:259, :] = channel_sum(lambda xl: cm[xl, 64:192, :])
    pack_out[259:260, :] = channel_sum(lambda xl: cf[xl])
    lane = iota((1, 128), 1)
    row = jnp.where(lane == 0, jnp.sum(cot_sum[0]), 0.0)
    row = jnp.where(lane == 1, jnp.sum(cot_sum[1]), row)
    pack_out[260:261, :] = jnp.where(lane == 2, jnp.sum(loss), row)
    core = place_ref[1]
    half = PACK_ROWS // 2
    mine_out[...] = pack_out[pl.ds(pl.multiple_of(core * half, 8), half), :]
    theirs_out[...] = pack_out[pl.ds(pl.multiple_of((1 - core) * half, 8), half), :]

    place = place_ref[0]
    start = 2 * (place % 4)
    high = place >= 4

    def pick(v):
        return jnp.where(high, v[:, 128:], v[:, :128])

    for x in range(2):
        field_out[x] = pick(own_field[start + x])
        rest_out[x] = pick(own_rest[start + x])
    for x in range(4):
        window_out[x] = pick(cf[start + x])
        partner_out[x] = pick(cf[start + x, pl.ds(pl.multiple_of((1 - core) * 64, 64), 64), :])
        beyond_out[x] = pick(cf[start + x, pl.ds(pl.multiple_of(core * 64, 64), 64), :])


def input_kernel(place_ref, partner_ref, beyond_ref, own_ref, taps_ref, rest_ref, out_ref, band):
    shape = (8, 128)
    upper = iota(shape, 0) < 4
    zero = jnp.zeros(shape, F32)
    for d in range(3):
        for window in range(4):
            for pair in range(2):
                tiles = []
                for x in range(2):
                    a = window - x
                    if 0 <= a <= 2:
                        taps = [taps_ref[d * 9 + a * 3 + b].astype(F32) for b in range(3)]
                        tiles.append(
                            jnp.where(
                                upper, band_tile(taps, 2 * pair, 8), band_tile(taps, 2 * pair - 1, 8)
                            )
                        )
                    else:
                        tiles.append(zero)
                lane = (window * 2 + pair) * 128
                band[d * 16 : d * 16 + 16, lane : lane + 128] = jnp.concatenate(tiles, axis=0).astype(BF16)
    low_core = place_ref[1] == 0
    left = jnp.where(low_core, beyond_ref[...], partner_ref[...])
    right = jnp.where(low_core, partner_ref[...], beyond_ref[...])
    window = jnp.concatenate([left, own_ref[...], right], axis=1).reshape(1024, 128)
    parts = jnp.dot(band[...], window, preferred_element_type=F32)
    out = pltpu.roll(parts[:16], 1, 1) + parts[16:32] + pltpu.roll(parts[32:], 127, 1)
    site = iota(shape, 0) // 4 + iota(shape, 0) % 4 + iota(shape, 1)
    for x in range(2):
        out_ref[x] = jnp.where((site + x) % 2 == 0, out[8 * x : 8 * x + 8], 0.0) + rest_ref[x]


def vmem():
    return pl.BlockSpec(memory_space=pltpu.VMEM)


def run_main(place, noise, small, selector, taps2, taps2t, taps3, b1, b2, b3):
    scratch = [
        ((XP, 4 * ROWS, 256), F32),
        ((3, XP, 4 * ROWS, 256), F32),
        ((XP, 768, 256), BF16),
        ((XP, 640, 256), BF16),
        ((XP, 256, 256), BF16),
        ((3, XP, 128, 256), BF16),
        ((XP, 128, 256), BF16),
        ((3, 2, XP, 24, 256), F32),
        ((2, 8, 32, 256), F32),
        ((XP, 32, 256), F32),
        ((8, 8, 256), F32),
        ((8, 8, 256), F32),
        ((256, 192), BF16),
        ((256, 384), BF16),
        ((384, 768), BF16),
        ((384, 768), BF16),
        ((192, 1536), BF16),
        ((1152, 256), F32),
        ((144, 256), F32),
        ((144, 128), F32),
        ((PACK_ROWS, 128), F32),
    ]
    return pl.pallas_call(
        main_kernel,
        out_shape=(
            jax.ShapeDtypeStruct((2, 8, 128), F32),
            jax.ShapeDtypeStruct((2, 8, 128), F32),
            jax.ShapeDtypeStruct((4, 128, 128), BF16),
            jax.ShapeDtypeStruct((4, 64, 128), BF16),
            jax.ShapeDtypeStruct((4, 64, 128), BF16),
            jax.ShapeDtypeStruct((PACK_ROWS // 2, 128), F32),
            jax.ShapeDtypeStruct((PACK_ROWS // 2, 128), F32),
        ),
        in_specs=[pl.BlockSpec(memory_space=pltpu.SMEM)] + [vmem()] * 9,
        out_specs=(vmem(),) * 7,
        scratch_shapes=[pltpu.VMEM(s, t) for s, t in scratch],
        compiler_params=pltpu.CompilerParams(vmem_limit_bytes=56 * 1024 * 1024),
    )(place, noise, small, selector, taps2, taps2t, taps3, b1, b2, b3)


def run_input(place, partner, beyond, own, taps, rest):
    return pl.pallas_call(
        input_kernel,
        out_shape=jax.ShapeDtypeStruct((2, 8, 128), F32),
        in_specs=[pl.BlockSpec(memory_space=pltpu.SMEM)] + [vmem()] * 5,
        out_specs=vmem(),
        scratch_shapes=[pltpu.VMEM((48, 1024), BF16)],
        compiler_params=pltpu.CompilerParams(vmem_limit_bytes=16 * 1024 * 1024),
    )(place, partner, beyond, own, taps, rest)


def unpack_kernel(scale, place_ref, mine_ref, theirs_ref, loss, first, b1, middle, b2, last, b3, both):
    core = place_ref[1]
    half = PACK_ROWS // 2
    both[pl.ds(pl.multiple_of(core * half, 8), half), :] = mine_ref[...] * scale
    both[pl.ds(pl.multiple_of((1 - core) * half, 8), half), :] = theirs_ref[...] * scale

    def lanes_from(v, start):
        return v if start == 0 else pltpu.roll(v, 128 - start, 1)

    for d in range(3):
        for j in range(3):
            a = 2 - j
            g = d * 3 + j
            most = both[g * 16 : g * 16 + 16, :]
            third = both[144 + (g // 2) * 16 : 160 + (g // 2) * 16, :]
            for b in range(3):
                for c in range(3):
                    if b < 2:
                        v = lanes_from(most, b * 64 + c * 16)
                    else:
                        v = lanes_from(third, (g % 2) * 64 + c * 16)
                    middle[a * 27 + b * 9 + c * 3 + d] = v[:, :16]
    for d in range(3):
        for a in range(3):
            g = d * 3 + a
            if g < 8:
                v = lanes_from(both[224:240, :], 16 * g)
            else:
                v = lanes_from(both[208:224, :], 64)
            for b in range(3):
                for c in range(3):
                    row = b * 4 + c
                    first[a * 9 + b * 3 + c, d : d + 1, :] = v[row : row + 1, :16]
    for b in range(3):
        for c in range(3):
            if b < 2:
                v = lanes_from(both[240:264, :], b * 64 + c * 16)
            else:
                v = lanes_from(both[264:288, :], c * 16)
            for d in range(3):
                for ch in range(2):
                    for a in range(3):
                        row = (2 - d) * 6 + ch * 3 + 2 - a
                        last[a * 27 + b * 9 + c * 3 + d, ch : ch + 1, :] = v[row : row + 1, :16]
    b2[...] = both[258:259, :16]
    b1[...] = both[259:260, :16]
    row = both[260:261, :]
    b3[...] = row[:, :2]
    loss[...] = pltpu.roll(row, 126, 1)[:, :1]


def run_unpack(scale, place, mine, theirs):
    shapes = ((1, 1), (27, 3, 16), (1, 16), (81, 16, 16), (1, 16), (81, 2, 16), (1, 2))
    return pl.pallas_call(
        functools.partial(unpack_kernel, scale),
        out_shape=tuple(jax.ShapeDtypeStruct(s, F32) for s in shapes),
        in_specs=[pl.BlockSpec(memory_space=pltpu.SMEM), vmem(), vmem()],
        out_specs=(vmem(),) * len(shapes),
        scratch_shapes=[pltpu.VMEM((PACK_ROWS, 128), F32)],
        compiler_params=pltpu.CompilerParams(vmem_limit_bytes=16 * 1024 * 1024),
    )(place, mine, theirs)


def pad_taps(v):
    return jnp.pad(v, [(0, 0)] * (v.ndim - 2) + [(0, 1), (0, 0)])


def hidden_taps(kernel):
    v = pad_taps(jnp.transpose(kernel, (5, 2, 3, 0, 4, 1))).reshape(27, 16, 64)
    return jnp.concatenate([v, v], axis=2)


def banded_taps(v):
    v = pad_taps(v)
    v = jnp.stack([jnp.roll(v, t - 1, axis=2) for t in range(4)], axis=2)
    v = v.reshape(27, -1, 64)
    return jnp.concatenate([v, v], axis=2)


def swapped(v, axis_size, partner):
    return lax.ppermute(v, "gy", [(i, partner(i)) for i in range(axis_size)])


def gather_noise(noise):
    size_y = lax.axis_size("gy")
    size_x = lax.axis_size("gx")
    even = lax.axis_index("gy") % 2 == 0
    chips = size_y // 2

    def far(i):
        return (i - 3) % size_y if i % 2 == 0 else (i + 3) % size_y

    def chip_after(i):
        return ((((i >> 1) + 1) ^ 1) - 1) % chips * 2 + (i & 1)

    beside = swapped(noise, size_y, lambda i: i ^ 1)
    near, beside = lax.optimization_barrier((noise, beside))
    distant = swapped(near, size_y, far)
    block = jnp.concatenate(
        [jnp.where(even, noise, beside), jnp.where(even, beside, noise)], axis=1
    )
    paired = swapped(block, size_y, lambda i: i ^ 2)
    across = swapped(block, size_y, chip_after)
    even_chip = (lax.axis_index("gy") // 2) % 2 == 0
    before = jnp.where(even_chip, across, paired)
    after = jnp.where(even_chip, paired, across)
    middle = jnp.concatenate([before, block, after], axis=1)
    window = jnp.where(
        even,
        jnp.concatenate([distant, middle], axis=1),
        jnp.concatenate([middle, distant], axis=1),
    )
    window = window.reshape(2, 4 * ROWS, 128)
    sent = jnp.broadcast_to(window[None], (size_x,) + window.shape)
    return lax.all_to_all(sent, "gx", 0, 0, tiled=True).reshape(16, 4 * ROWS, 128)


def sum_over_y(mine, theirs):
    size_y = lax.axis_size("gy")

    def along_z(partner):
        def f(i):
            return ((i >> 4) * 8 + partner((i >> 1) & 7)) * 2 + (i & 1)

        return f

    crossing = (3, 6, 5, 0, 7, 2, 1, 4)
    v = mine + swapped(theirs, size_y, lambda i: i ^ 1)
    for partner in (
        lambda i: i ^ 16,
        along_z(lambda z: z ^ 1),
        along_z(lambda z: (((z + 1) ^ 1) - 1) % 8),
        along_z(lambda z: crossing[z]),
    ):
        v = v + swapped(v, size_y, partner)
    return v, swapped(v, size_y, lambda i: i ^ 1)


def local(noise, w_first, b_first, w_middle, b_middle, w_last, b_last):
    size_y = lax.axis_size("gy")
    sites = float(noise.size * lax.axis_size("gx") * size_y)
    flip = (slice(None), slice(None)) + (slice(None, None, -1),) * 4
    small = jnp.concatenate(
        [
            jnp.transpose(w_first[:, 0], (4, 0, 1, 2, 3)).reshape(48, 27),
            jnp.transpose(w_last[flip], (5, 0, 1, 2, 3, 4)).reshape(96, 27),
        ],
        axis=0,
    )
    small = jnp.pad(small, ((0, 0), (0, 5)))
    taps2 = hidden_taps(w_middle)
    taps2t = hidden_taps(jnp.transpose(w_middle[flip], (1, 0, 2, 3, 4, 5)))
    taps3 = banded_taps(jnp.transpose(w_last, (5, 2, 3, 0, 4, 1)).reshape(27, 2, 3, 16))
    tapsd = banded_taps(jnp.transpose(w_first[flip], (5, 2, 3, 1, 4, 0)).reshape(27, 1, 3, 16))
    tapsd = jnp.concatenate([tapsd, tapsd], axis=1)

    gathered = gather_noise(noise)
    place = jnp.stack([lax.axis_index("gx"), lax.axis_index("gy") % 2]).astype(jnp.int32)
    field, rest, window, to_partner, to_beyond, mine, theirs = run_main(
        place,
        gathered,
        small,
        jnp.asarray(tap_selector(), BF16),
        taps2,
        taps2t,
        taps3,
        b_first.reshape(16, 1),
        b_middle.reshape(16, 1),
        jnp.repeat(b_last, 4).reshape(8, 1),
    )
    partner = swapped(to_partner, size_y, lambda i: i ^ 1)
    beyond = swapped(to_beyond, size_y, lambda i: (((i + 1) ^ 1) - 1) % size_y)
    noise_grad = run_input(place, partner, beyond, window, tapsd, rest)

    mine, theirs = sum_over_y(mine, theirs)
    loss, first, b1, middle, b2, last, b3 = run_unpack(1.0 / sites, place, mine, theirs)
    return (
        field.reshape(noise.shape),
        noise_grad.reshape(noise.shape),
        loss.reshape(()),
        jnp.transpose(first.reshape(3, 3, 3, 3, 16), (4, 0, 1, 2, 3))[:, None],
        b1.reshape(16),
        jnp.transpose(middle.reshape(3, 3, 3, 3, 16, 16), (4, 5, 0, 1, 2, 3)),
        b2.reshape(16),
        jnp.transpose(last.reshape(3, 3, 3, 3, 2, 16), (4, 5, 0, 1, 2, 3)),
        b3.reshape(2),
    )


def solution(mesh):
    placed = (P("gx", "gy", None, None), P(), P(), P(), P(), P(), P())
    return jax.shard_map(
        local,
        mesh=mesh,
        in_specs=placed,
        out_specs=(P("gx", "gy", None, None), P("gx", "gy", None, None)) + (P(),) * 7,
        check_vma=False,
    )
```

```python
import functools

import jax
import jax.numpy as jnp
import numpy as np
from jax import lax
from jax.experimental import pallas as pl
from jax.experimental.pallas import tpu as pltpu
from jax.sharding import PartitionSpec as P

HOPPING = 0.15
QUARTIC = 0.1
F32 = jnp.float32
BF16 = jnp.bfloat16

HALO = 6
ROWS = 2 + 2 * HALO
XP = 10
PACK_ROWS = 288
GROUP = 8


def tap_selector():
    table = np.zeros((32, 16, 64), np.float32)
    for x in range(2):
        for y in range(2):
            for t in range(4):
                for a in range(3):
                    for b in range(3):
                        for c in range(3):
                            column = (x + a) * 16 + (y + b) * 4 + (t + c - 1) % 4
                            table[a * 9 + b * 3 + c, (x * 2 + y) * 4 + t, column] = 1.0
    return table.reshape(32, 1024)


def roll_z(v, shift):
    shift = shift % 128
    if shift == 0:
        return v
    last = v.ndim - 1
    return jnp.concatenate(
        [pltpu.roll(v[..., :128], shift, last), pltpu.roll(v[..., 128:], shift, last)], axis=last
    )


def swap_halves(v):
    return jnp.concatenate([v[..., 128:], v[..., :128]], axis=v.ndim - 1)


def iota(shape, dim):
    return lax.broadcasted_iota(jnp.int32, shape, dim)


def band_tile(taps, first, rows):
    zero = jnp.zeros((rows, 128), F32)
    left = taps[first] if 0 <= first <= 2 else zero
    right = taps[first + 1] if 0 <= first + 1 <= 2 else zero
    return jnp.where(iota((rows, 128), 1) < 64, left, right)


def build_hidden_band(taps_ref, band_ref):
    for d in range(3):
        for t in range(4):
            for a in range(3):
                taps = []
                for b in range(3):
                    tap = taps_ref[d * 9 + a * 3 + b].astype(F32)
                    taps.append(pltpu.roll(tap, (16 * (t - 1)) % 128, 1))
                for y in range(2):
                    for pair in range(2):
                        row = d * 128 + (y * 4 + t) * 16
                        lane = (a * 2 + pair) * 128
                        tile = band_tile(taps, 2 * pair - y, 16)
                        band_ref[row : row + 16, lane : lane + 128] = tile.astype(BF16)


def build_head_band(taps_ref, band_ref):
    for d in range(3):
        for x in range(2):
            for window in range(4):
                a = window - x
                for pair in range(3):
                    for half in range(2):
                        row = d * 64 + x * 32 + half * 16
                        lane = (window * 3 + pair) * 128
                        if 0 <= a <= 2:
                            taps = [taps_ref[d * 9 + a * 3 + b].astype(F32) for b in range(3)]
                            tile = jnp.concatenate(
                                [band_tile(taps, 2 * pair - 2 * half - y, 8) for y in range(2)], axis=0
                            )
                        else:
                            tile = jnp.zeros((16, 128), F32)
                        band_ref[row : row + 16, lane : lane + 128] = tile.astype(BF16)


def combine_z(parts, rows):
    return (
        roll_z(parts[:rows], 1) + parts[rows : 2 * rows] + roll_z(parts[2 * rows :], -1)
    )


def rotate_groups(v, step, lanes):
    if step == 0:
        return v
    group = (iota(v.shape, 1) // lanes) % 4
    ahead = pltpu.roll(v, (128 - lanes * step) % 128, 1)
    behind = pltpu.roll(v, lanes * (4 - step), 1)
    return jnp.where(group + step < 4, ahead, behind)


def rotate_rows(v, step):
    if step == 0:
        return v
    ahead = pltpu.roll(v, v.shape[0] - step, 0)
    behind = pltpu.roll(v, 4 - step, 0)
    return jnp.where(iota(v.shape, 0) % 4 + step < 4, ahead, behind)


def main_kernel(
    noise_ref,
    small_ref,
    selector_ref,
    taps2_ref,
    taps2t_ref,
    taps3_ref,
    b1_ref,
    b2_ref,
    b3_ref,
    parts_out,
    window_out,
    partner_out,
    beyond_out,
    mine_out,
    theirs_out,
    nz,
    inp,
    h1,
    h2,
    cm,
    cmr,
    cf,
    cl,
    head,
    phi,
    own_parts,
    w1,
    wl,
    w2,
    w2t,
    w3,
    gm,
    gl,
    gf,
    pack_out,
    raw,
    raw_sem,
):
    arriving = pltpu.make_async_copy(noise_ref, raw, raw_sem)
    arriving.start()

    def column(ref, rows, repeats):
        shape = (rows * repeats, rows)
        match = iota(shape, 0) // repeats == iota(shape, 1)
        return jnp.sum(jnp.where(match, ref[...], 0.0), axis=1, keepdims=True)

    b1 = column(b1_ref, 16, 1)
    b2 = column(b2_ref, 16, 1)
    b3 = column(b3_ref, 2, 4)

    spread = jnp.dot(small_ref[...], selector_ref[...], preferred_element_type=F32)
    for g in range(16):
        piece = spread[:, g * 64 : (g + 1) * 64]
        w1[g * 16 : (g + 1) * 16, :] = jnp.concatenate(
            [piece[16 * k : 16 * k + 16] for k in range(3)], axis=1
        ).astype(BF16)
        wl[g * 16 : (g + 1) * 16, :] = jnp.concatenate(
            [piece[48 + 16 * k : 64 + 16 * k] for k in range(6)], axis=1
        ).astype(BF16)
    build_hidden_band(taps2_ref, w2)
    build_hidden_band(taps2t_ref, w2t)
    build_head_band(taps3_ref, w3)

    arriving.wait()

    rows_in = 4 * ROWS
    shape = (rows_in, 256)
    site = iota(shape, 0) // 4 + iota(shape, 0) % 4 + iota(shape, 1) % 128
    even = site % 2
    for xl in range(8):
        v = jnp.concatenate([raw[xl], raw[xl + 8]], axis=1).astype(F32)
        nz[xl + 1] = v
        if xl == 7:
            nz[0] = swap_halves(v)
        if xl == 0:
            nz[9] = swap_halves(v)
    for xl in range(XP):
        v = jnp.where(even == (xl + 1) % 2, nz[xl], 0.0)
        inp[0, xl] = roll_z(v, 1)
        inp[1, xl] = v
        inp[2, xl] = roll_z(v, -1)

    def wrap(ref):
        ref[0] = swap_halves(ref[8])
        ref[9] = swap_halves(ref[1])

    def first_body(step, _):
        xp = step // 6
        yp = step % 6
        window = inp[:, pl.ds(2 * xp, 4), pl.ds(pl.multiple_of(8 * yp, 8), 16), :]
        window = window.reshape(192, 256).astype(BF16)
        out = jnp.dot(w1[...], window, preferred_element_type=F32)
        out = jnp.tanh(out.reshape(16, 16, 256) + b1[None]).reshape(256, 256).astype(BF16)
        row = pl.ds(pl.multiple_of(yp * 128, 128), 128)
        h1[2 * xp + 1, row, :] = out[:128]
        h1[2 * xp + 2, row, :] = out[128:]
        return 0

    lax.fori_loop(0, 24, first_body, 0, unroll=12)
    wrap(h1)

    def second_body(step, _):
        xl = step // 5
        yp = step % 5
        window = h1[pl.ds(xl, 3), pl.ds(pl.multiple_of(yp * 128, 128), 256), :].reshape(768, 256)
        parts = jnp.dot(w2[...], window, preferred_element_type=F32)
        out = combine_z(parts, 128)
        out = jnp.tanh(out.reshape(8, 16, 256) + b2[None]).reshape(128, 256)
        h2[xl + 1, pl.ds(pl.multiple_of(yp * 128, 128), 128), :] = out.astype(BF16)
        return 0

    lax.fori_loop(0, 40, second_body, 0, unroll=20)
    wrap(h2)

    top = iota((8, 256), 0) < 4

    def head_body(step, _):
        xp = step // 2
        yq = step % 2
        window = h2[pl.ds(2 * xp, 4), pl.ds(pl.multiple_of(yq * 256, 256), 384), :].reshape(1536, 256)
        parts = jnp.dot(w3[...], window, preferred_element_type=F32)
        out = combine_z(parts, 64)
        out = (out.reshape(8, 8, 256) + b3[None]).reshape(64, 256)
        for x in range(2):
            for pair in range(2):
                base = x * 32 + pair * 16
                lower = out[base : base + 8]
                upper = out[base + 8 : base + 16]
                row = pl.ds(pl.multiple_of(yq * 16, 16) + pair * 8, 8)
                head[0, 2 * xp + x, row, :] = jnp.where(top, lower, pltpu.roll(upper, 4, 0))
                head[1, 2 * xp + x, row, :] = jnp.where(top, pltpu.roll(lower, 4, 0), upper)
        return 0

    lax.fori_loop(0, 8, head_body, 0, unroll=8)

    shape = (32, 256)
    row32 = iota(shape, 0)
    site = row32 // 4 + 1 + row32 % 4 + iota(shape, 1) % 128
    even = site % 2
    for xl in range(8):
        frozen = even == xl % 2
        noise = nz[xl + 1, 12:44, :]
        log_scale = jnp.tanh(head[0, xl])
        head[0, xl] = log_scale
        moved = noise * jnp.exp(log_scale) + head[1, xl]
        phi[xl + 1] = jnp.where(frozen, noise, moved)
    wrap(phi)

    own = (row32 >= 12) & (row32 < 20)
    inner_t = row32 % 4
    loss = jnp.zeros(shape, F32)
    cot_sum = [jnp.zeros((8, 256), F32), jnp.zeros((8, 256), F32)]
    for xl in range(8):
        frozen = even == xl % 2
        noise = nz[xl + 1, 12:44, :]
        log_scale = head[0, xl]
        growth = jnp.exp(log_scale)
        here = phi[xl + 1]
        upward = (
            phi[xl + 2]
            + pltpu.roll(here, 28, 0)
            + jnp.where(inner_t == 3, pltpu.roll(here, 3, 0), pltpu.roll(here, 31, 0))
            + roll_z(here, -1)
        )
        downward = (
            phi[xl]
            + pltpu.roll(here, 4, 0)
            + jnp.where(inner_t == 0, pltpu.roll(here, 29, 0), pltpu.roll(here, 1, 0))
            + roll_z(here, 1)
        )
        squared = here * here
        density = (
            -2.0 * HOPPING * here * upward + squared + QUARTIC * (squared - 1.0) * (squared - 1.0)
        )
        local = -0.5 * noise * noise - jnp.where(frozen, 0.0, log_scale) + density
        loss = loss + jnp.where(own, local, 0.0)
        force = (
            -2.0 * HOPPING * (upward + downward)
            + 2.0 * here
            + 4.0 * QUARTIC * here * (squared - 1.0)
        )
        d_scale = (force * noise * growth - 1.0) * (1.0 - log_scale * log_scale)
        pair = (jnp.where(frozen, 0.0, d_scale), jnp.where(frozen, 0.0, force))
        own_parts[0, xl] = growth[12:20]
        own_parts[1, xl] = head[1, xl][12:20]
        own_parts[2, xl] = (upward + downward)[12:20]
        for ch in range(2):
            v = pltpu.roll(pair[ch], 28, 0)[:24].astype(BF16).astype(F32)
            cot_sum[ch] = cot_sum[ch] + v[8:16]
            for d, shift in ((0, 1), (1, 0), (2, -1)):
                moved = roll_z(v, shift)
                cl[d, ch, xl + 1] = moved
                if xl == 7:
                    cl[d, ch, 0] = swap_halves(moved)
                if xl == 0:
                    cl[d, ch, 9] = swap_halves(moved)

    def middle_body(step, _):
        xp = step // 2
        yp = step % 2
        window = cl[:, :, pl.ds(2 * xp, 4), pl.ds(pl.multiple_of(8 * yp, 8), 16), :]
        window = window.reshape(384, 256).astype(BF16)
        out = jnp.dot(wl[...], window, preferred_element_type=F32)
        for x in range(2):
            hidden = h2[2 * xp + 1 + x, pl.ds(pl.multiple_of((3 + 2 * yp) * 64, 64), 128), :].astype(F32)
            v = out[128 * x : 128 * x + 128] * (1.0 - hidden * hidden)
            cm[2 * xp + 1 + x, pl.ds(pl.multiple_of(yp * 128, 128), 128), :] = v.astype(BF16)
        return 0

    lax.fori_loop(0, 8, middle_body, 0, unroll=8)
    wrap(cm)

    def shift_body(xl, _):
        v = cm[xl, 64:192, :].astype(F32)
        cmr[0, xl] = roll_z(v, -1).astype(BF16)
        cmr[1, xl] = v.astype(BF16)
        cmr[2, xl] = roll_z(v, 1).astype(BF16)
        return 0

    lax.fori_loop(0, XP, shift_body, 0, unroll=5)

    def first_cot_body(xl, _):
        window = cm[pl.ds(xl, 3)].reshape(768, 256)
        parts = jnp.dot(w2t[...], window, preferred_element_type=F32)
        out = combine_z(parts, 128)
        hidden = h1[xl + 1, 320:448, :].astype(F32)
        cf[xl + 1] = (out * (1.0 - hidden * hidden)).astype(BF16)
        return 0

    lax.fori_loop(0, 8, first_cot_body, 0, unroll=8)
    wrap(cf)

    gm[...] = jnp.zeros_like(gm)
    gl[...] = jnp.zeros_like(gl)
    gf[...] = jnp.zeros_like(gf)
    over_lanes = (((1,), (1,)), ((), ()))

    def grad_body(step, _):
        xs = [GROUP * step + 1 + k for k in range(GROUP)]

        def along(parts):
            return jnp.concatenate(parts, axis=1)

        left = along([cmr[:, pl.ds(x - 1, 3)].reshape(1152, 256) for x in xs])
        right = along([h1[x, 256:512, :] for x in xs])
        gm[...] += lax.dot_general(left, right, over_lanes, preferred_element_type=F32)
        left = along([cl[:, :, pl.ds(x - 1, 3), 8:16, :].reshape(144, 256).astype(BF16) for x in xs])
        right = along([h2[x, 192:448, :] for x in xs])
        gl[...] += lax.dot_general(left, right, over_lanes, preferred_element_type=F32)
        left = along([inp[:, pl.ds(x - 1, 3), 20:36, :].reshape(144, 256).astype(BF16) for x in xs])
        right = along([cf[x] for x in xs])
        gf[...] += lax.dot_general(left, right, over_lanes, preferred_element_type=F32)
        return 0

    lax.fori_loop(0, 8 // GROUP, grad_body, 0)

    low = iota((16, 128), 1) < 64
    third = []
    for g in range(9):
        sums = []
        for y in range(2):
            for side in range(2):
                total = None
                for t in range(4):
                    row = g * 128 + y * 64 + t * 16
                    block = gm[row : row + 16, side * 128 : side * 128 + 128]
                    block = rotate_groups(block, (t - 1) % 4, 16)
                    total = block if total is None else total + block
                sums.append(total)
        u0, u1, v0, v1 = sums
        v0 = pltpu.roll(v0, 64, 1)
        v1 = pltpu.roll(v1, 64, 1)
        pack_out[g * 16 : g * 16 + 16, :] = u0 + jnp.where(low, v0, v1)
        third.append(u1 + v1)
    v = gf[...]
    shape = (144, 128)
    total = jnp.zeros(shape, F32)
    for y in range(2):
        for t in range(4):
            moved = v if y + t == 0 else pltpu.roll(v, 128 - (y * 64 + t * 16), 1)
            if y:
                moved = pltpu.roll(moved, 140, 0)
            total = total + rotate_rows(moved, (t - 1) % 4)
    total = jnp.where(iota(shape, 1) < 16, total, 0.0)
    packed = total[:16]
    for g in range(1, 8):
        packed = packed + pltpu.roll(total[g * 16 : g * 16 + 16], 16 * g, 1)
    pack_out[224:240, :] = packed
    third.append(total[128:144])
    for g in range(5):
        packed = jnp.where(low, third[2 * g], pltpu.roll(third[2 * g + 1], 64, 1))
        pack_out[144 + g * 16 : 160 + g * 16, :] = packed

    shape = (144, 128)
    row144 = iota(shape, 0)
    sides = []
    for side in range(2):
        v = gl[:, side * 128 : side * 128 + 128]
        total = jnp.zeros(shape, F32)
        for t in range(4):
            total = total + jnp.where(row144 % 4 == t, rotate_groups(v, (t - 1) % 4, 16), 0.0)
        sides.append(total)
    lower_y = (row144 // 4) % 2 == 0
    r0, r1 = sides
    s0 = pltpu.roll(r0, 64, 1)
    s1 = pltpu.roll(r1, 64, 1)
    low = iota(shape, 1) < 64
    both = jnp.where(lower_y, r0, jnp.where(low, s0, s1))
    last = jnp.where(lower_y, r1, s1)
    pack_out[240:288, :] = jnp.zeros((48, 128), F32)
    pack_out[240:258, :] = both.reshape(18, 8, 128).sum(axis=1)
    pack_out[264:282, :] = last.reshape(18, 8, 128).sum(axis=1)

    diagonal = iota((16, 128), 0) == iota((16, 128), 1)

    def channel_sum(read):
        acc = None
        for xl in range(1, 9):
            v = read(xl).astype(F32)
            v = v[:, :128] + v[:, 128:]
            acc = v if acc is None else acc + v
        acc = jnp.sum(acc.reshape(8, 16, 128).sum(axis=0), axis=1, keepdims=True)
        return jnp.sum(jnp.where(diagonal, acc, 0.0), axis=0, keepdims=True)

    pack_out[258:259, :] = channel_sum(lambda xl: cm[xl, 64:192, :])
    pack_out[259:260, :] = channel_sum(lambda xl: cf[xl])
    lane = iota((1, 128), 1)
    row = jnp.where(lane == 0, jnp.sum(cot_sum[0]), 0.0)
    row = jnp.where(lane == 1, jnp.sum(cot_sum[1]), row)
    pack_out[260:261, :] = jnp.where(lane == 2, jnp.sum(loss), row)
    core = lax.rem(lax.axis_index("gy"), 2)
    half = PACK_ROWS // 2
    mine_out[...] = pack_out[pl.ds(pl.multiple_of(core * half, 8), half), :]
    theirs_out[...] = pack_out[pl.ds(pl.multiple_of((1 - core) * half, 8), half), :]

    place = lax.axis_index("gx")
    start = 2 * (place % 4)
    high = place >= 4

    def pick(v):
        return jnp.where(high, v[:, 128:], v[:, :128])

    for x in range(2):
        for k in range(3):
            parts_out[k, x] = pick(own_parts[k, start + x])
    for x in range(4):
        window_out[x] = pick(cf[start + x])
        partner_out[x] = pick(cf[start + x, pl.ds(pl.multiple_of((1 - core) * 64, 64), 64), :])
        beyond_out[x] = pick(cf[start + x, pl.ds(pl.multiple_of(core * 64, 64), 64), :])


def input_kernel(
    partner_ref, beyond_ref, own_ref, taps_ref, parts_ref, noise_ref, field_ref, out_ref, band
):
    shape = (8, 128)
    upper = iota(shape, 0) < 4
    zero = jnp.zeros(shape, F32)
    for d in range(3):
        for window in range(4):
            for pair in range(2):
                tiles = []
                for x in range(2):
                    a = window - x
                    if 0 <= a <= 2:
                        taps = [taps_ref[d * 9 + a * 3 + b].astype(F32) for b in range(3)]
                        tiles.append(
                            jnp.where(
                                upper, band_tile(taps, 2 * pair, 8), band_tile(taps, 2 * pair - 1, 8)
                            )
                        )
                    else:
                        tiles.append(zero)
                lane = (window * 2 + pair) * 128
                band[d * 16 : d * 16 + 16, lane : lane + 128] = jnp.concatenate(tiles, axis=0).astype(BF16)
    low_core = lax.rem(lax.axis_index("gy"), 2) == 0
    left = jnp.where(low_core, beyond_ref[...], partner_ref[...])
    right = jnp.where(low_core, partner_ref[...], beyond_ref[...])
    window = jnp.concatenate([left, own_ref[...], right], axis=1).reshape(1024, 128)
    parts = jnp.dot(band[...], window, preferred_element_type=F32)
    out = pltpu.roll(parts[:16], 1, 1) + parts[16:32] + pltpu.roll(parts[32:], 127, 1)
    site = iota(shape, 0) // 4 + iota(shape, 0) % 4 + iota(shape, 1)
    for x in range(2):
        frozen = (site + x) % 2 == 0
        noise = noise_ref[x]
        growth = parts_ref[0, x]
        here = jnp.where(frozen, noise, noise * growth + parts_ref[1, x])
        force = (
            -2.0 * HOPPING * parts_ref[2, x]
            + 2.0 * here
            + 4.0 * QUARTIC * here * (here * here - 1.0)
        )
        field_ref[x] = here
        out_ref[x] = jnp.where(frozen, out[8 * x : 8 * x + 8] + force, force * growth) - noise


def vmem():
    return pl.BlockSpec(memory_space=pltpu.VMEM)


def run_main(noise, small, selector, taps2, taps2t, taps3, b1, b2, b3):
    scratch = [
        ((XP, 4 * ROWS, 256), F32),
        ((3, XP, 4 * ROWS, 256), F32),
        ((XP, 768, 256), BF16),
        ((XP, 640, 256), BF16),
        ((XP, 256, 256), BF16),
        ((3, XP, 128, 256), BF16),
        ((XP, 128, 256), BF16),
        ((3, 2, XP, 24, 256), F32),
        ((2, 8, 32, 256), F32),
        ((XP, 32, 256), F32),
        ((3, 8, 8, 256), F32),
        ((256, 192), BF16),
        ((256, 384), BF16),
        ((384, 768), BF16),
        ((384, 768), BF16),
        ((192, 1536), BF16),
        ((1152, 256), F32),
        ((144, 256), F32),
        ((144, 128), F32),
        ((PACK_ROWS, 128), F32),
        ((16, 4 * ROWS, 128), BF16),
    ]
    return pl.pallas_call(
        main_kernel,
        out_shape=(
            jax.ShapeDtypeStruct((3, 2, 8, 128), F32),
            jax.ShapeDtypeStruct((4, 128, 128), BF16),
            jax.ShapeDtypeStruct((4, 64, 128), BF16),
            jax.ShapeDtypeStruct((4, 64, 128), BF16),
            jax.ShapeDtypeStruct((PACK_ROWS // 2, 128), F32),
            jax.ShapeDtypeStruct((PACK_ROWS // 2, 128), F32),
        ),
        in_specs=[pl.BlockSpec(memory_space=pltpu.HBM)] + [vmem()] * 8,
        out_specs=(vmem(),) * 6,
        scratch_shapes=[pltpu.VMEM(s, t) for s, t in scratch] + [pltpu.SemaphoreType.DMA],
        compiler_params=pltpu.CompilerParams(vmem_limit_bytes=56 * 1024 * 1024),
    )(noise, small, selector, taps2, taps2t, taps3, b1, b2, b3)


def window_kernel(copies, distant_ref, block_ref, paired_ref, across_ref, out_ref):
    me = lax.axis_index("gy")
    even = lax.rem(me, 2) == 0
    even_chip = lax.rem(me // 2, 2) == 0
    for x in range(2):
        before = jnp.where(even_chip, across_ref[x], paired_ref[x])
        after = jnp.where(even_chip, paired_ref[x], across_ref[x])
        tiles = [before[:8], before[8:], block_ref[x, :8], block_ref[x, 8:], after[:8], after[8:]]
        distant = distant_ref[x]
        rows = [jnp.where(even, distant, tiles[0])]
        rows += [jnp.where(even, tiles[k - 1], tiles[k]) for k in range(1, 6)]
        rows += [jnp.where(even, tiles[5], distant)]
        window = jnp.concatenate(rows, axis=0).astype(BF16)
        for k in range(copies):
            out_ref[k, x] = window


def run_window(distant, block, paired, across):
    copies = lax.axis_size("gx")
    return pl.pallas_call(
        functools.partial(window_kernel, copies),
        out_shape=jax.ShapeDtypeStruct((copies, 2, 4 * ROWS, 128), BF16),
        in_specs=[vmem()] * 4,
        out_specs=vmem(),
        compiler_params=pltpu.CompilerParams(vmem_limit_bytes=16 * 1024 * 1024),
    )(distant, block, paired, across)


def run_input(partner, beyond, own, taps, parts, noise):
    return pl.pallas_call(
        input_kernel,
        out_shape=(jax.ShapeDtypeStruct((2, 8, 128), F32),) * 2,
        in_specs=[vmem()] * 6,
        out_specs=(vmem(),) * 2,
        scratch_shapes=[pltpu.VMEM((48, 1024), BF16)],
        compiler_params=pltpu.CompilerParams(vmem_limit_bytes=16 * 1024 * 1024),
    )(partner, beyond, own, taps, parts, noise)


def unpack_kernel(scale, mine_ref, theirs_ref, loss, first, b1, middle, b2, last, b3, both):
    core = lax.rem(lax.axis_index("gy"), 2)
    half = PACK_ROWS // 2
    both[pl.ds(pl.multiple_of(core * half, 8), half), :] = mine_ref[...] * scale
    both[pl.ds(pl.multiple_of((1 - core) * half, 8), half), :] = theirs_ref[...] * scale

    def lanes_from(v, start):
        return v if start == 0 else pltpu.roll(v, 128 - start, 1)

    for d in range(3):
        for j in range(3):
            a = 2 - j
            g = d * 3 + j
            most = both[g * 16 : g * 16 + 16, :]
            third = both[144 + (g // 2) * 16 : 160 + (g // 2) * 16, :]
            for b in range(3):
                for c in range(3):
                    if b < 2:
                        v = lanes_from(most, b * 64 + c * 16)
                    else:
                        v = lanes_from(third, (g % 2) * 64 + c * 16)
                    middle[a * 27 + b * 9 + c * 3 + d] = v[:, :16]
    for d in range(3):
        for a in range(3):
            g = d * 3 + a
            if g < 8:
                v = lanes_from(both[224:240, :], 16 * g)
            else:
                v = lanes_from(both[208:224, :], 64)
            for b in range(3):
                for c in range(3):
                    row = b * 4 + c
                    first[a * 27 + b * 9 + c * 3 + d] = v[row : row + 1, :16]
    for b in range(3):
        for c in range(3):
            if b < 2:
                v = lanes_from(both[240:264, :], b * 64 + c * 16)
            else:
                v = lanes_from(both[264:288, :], c * 16)
            for d in range(3):
                for ch in range(2):
                    for a in range(3):
                        row = (2 - d) * 6 + ch * 3 + 2 - a
                        last[a * 27 + b * 9 + c * 3 + d, ch : ch + 1, :] = v[row : row + 1, :16]
    b2[...] = both[258:259, :16]
    b1[...] = both[259:260, :16]
    row = both[260:261, :]
    b3[...] = row[:, :2]
    loss[...] = pltpu.roll(row, 126, 1)[:, :1]


def run_unpack(scale, mine, theirs):
    shapes = ((1, 1), (81, 1, 16), (1, 16), (81, 16, 16), (1, 16), (81, 2, 16), (1, 2))
    return pl.pallas_call(
        functools.partial(unpack_kernel, scale),
        out_shape=tuple(jax.ShapeDtypeStruct(s, F32) for s in shapes),
        in_specs=[vmem(), vmem()],
        out_specs=(vmem(),) * len(shapes),
        scratch_shapes=[pltpu.VMEM((PACK_ROWS, 128), F32)],
        compiler_params=pltpu.CompilerParams(vmem_limit_bytes=16 * 1024 * 1024),
    )(mine, theirs)


def pad_taps(v):
    return jnp.pad(v, [(0, 0)] * (v.ndim - 2) + [(0, 1), (0, 0)])


def taps_kernel(kernel_ref, taps_ref, flipped_ref, spread):
    shape = (16, 128)
    lane = iota(shape, 1)
    group = (lane // 16) % 4
    repeat = jnp.where(iota(shape, 0) == lane % 16, 1.0, 0.0).astype(BF16)
    spread[...] = jnp.dot(kernel_ref[...], repeat, preferred_element_type=F32)
    unit = jnp.where(iota((16, 16), 0) == iota((16, 16), 1), 1.0, 0.0).astype(BF16)
    starts = [128 * k for k in range(10)] + [1168]
    turned = [
        lax.dot_general(
            unit, kernel_ref[k : k + 128, :], (((1,), (1,)), ((), ())), preferred_element_type=F32
        )
        for k in starts
    ]
    zero = jnp.zeros(shape, F32)
    for d in range(3):
        for a in range(3):
            for b in range(3):
                plain = zero
                flipped = zero
                for c in range(3):
                    tap = a * 27 + b * 9 + c * 3 + d
                    plain = jnp.where(group == c, spread[tap * 16 : tap * 16 + 16, :], plain)
                    tap = 80 - tap
                    chunk = tap // 8
                    offset = tap * 16 - starts[chunk]
                    shift = (c * 16 - offset) % 128
                    v = turned[chunk]
                    v = pltpu.roll(v, shift, 1) if shift else v
                    flipped = jnp.where(lane // 16 == c, v, flipped)
                flipped = flipped + pltpu.roll(flipped, 64, 1)
                taps_ref[d * 9 + a * 3 + b] = plain.astype(BF16)
                flipped_ref[d * 9 + a * 3 + b] = flipped.astype(BF16)


def hidden_taps(kernel):
    return pl.pallas_call(
        taps_kernel,
        out_shape=(jax.ShapeDtypeStruct((27, 16, 128), BF16),) * 2,
        in_specs=[vmem()],
        out_specs=(vmem(),) * 2,
        scratch_shapes=[pltpu.VMEM((1296, 128), F32)],
        compiler_params=pltpu.CompilerParams(vmem_limit_bytes=16 * 1024 * 1024),
    )(jnp.transpose(kernel, (2, 3, 4, 5, 0, 1)).reshape(1296, 16))


def banded_taps(v):
    v = pad_taps(v)
    v = jnp.stack([jnp.roll(v, t - 1, axis=2) for t in range(4)], axis=2)
    v = v.reshape(27, -1, 64)
    return jnp.concatenate([v, v], axis=2)


def swapped(v, axis_size, partner):
    return lax.ppermute(v, "gy", [(i, partner(i)) for i in range(axis_size)])


def gather_y(noise, weights):
    size_y = lax.axis_size("gy")
    even = lax.axis_index("gy") % 2 == 0
    chips = size_y // 2

    def far(i):
        return (i - 3) % size_y if i % 2 == 0 else (i + 3) % size_y

    def chip_after(i):
        return ((((i >> 1) + 1) ^ 1) - 1) % chips * 2 + (i & 1)

    distant = swapped(noise, size_y, far)
    beside = swapped(noise, size_y, lambda i: i ^ 1)
    block = jnp.concatenate(
        [jnp.where(even, noise, beside), jnp.where(even, beside, noise)], axis=1
    )
    block, *weights = lax.optimization_barrier((block, *weights))
    paired = swapped(block, size_y, lambda i: i ^ 2)
    across = swapped(block, size_y, chip_after)
    return run_window(
        distant.reshape(2, 8, 128),
        block.reshape(2, 16, 128),
        paired.reshape(2, 16, 128),
        across.reshape(2, 16, 128),
    ), weights


def sum_over_y(mine, theirs, *before_last):
    size_y = lax.axis_size("gy")

    def along_z(partner):
        def f(i):
            return ((i >> 4) * 8 + partner((i >> 1) & 7)) * 2 + (i & 1)

        return f

    crossing = (3, 6, 5, 0, 7, 2, 1, 4)
    v = mine + swapped(theirs, size_y, lambda i: i ^ 1)
    for partner in (
        lambda i: i ^ 16,
        along_z(lambda z: z ^ 1),
        along_z(lambda z: (((z + 1) ^ 1) - 1) % 8),
    ):
        v = v + swapped(v, size_y, partner)
    v, *before_last = lax.optimization_barrier((v, *before_last))
    v = v + swapped(v, size_y, along_z(lambda z: crossing[z]))
    return v, before_last


def local(noise, w_first, b_first, w_middle, b_middle, w_last, b_last):
    size_y = lax.axis_size("gy")
    sites = float(noise.size * lax.axis_size("gx") * size_y)
    sent, (w_first, w_middle, w_last) = gather_y(noise, (w_first, w_middle, w_last))
    gathered = lax.all_to_all(sent, "gx", 0, 0, tiled=True).reshape(16, 4 * ROWS, 128)
    flip = (slice(None), slice(None)) + (slice(None, None, -1),) * 4
    small = jnp.concatenate(
        [
            jnp.transpose(w_first[:, 0], (4, 0, 1, 2, 3)).reshape(48, 27),
            jnp.transpose(w_last[flip], (5, 0, 1, 2, 3, 4)).reshape(96, 27),
        ],
        axis=0,
    )
    small = jnp.pad(small, ((0, 0), (0, 5)))
    taps2, taps2t = hidden_taps(w_middle)
    taps3 = banded_taps(jnp.transpose(w_last, (5, 2, 3, 0, 4, 1)).reshape(27, 2, 3, 16))
    tapsd = banded_taps(jnp.transpose(w_first[flip], (5, 2, 3, 1, 4, 0)).reshape(27, 1, 3, 16))
    tapsd = jnp.concatenate([tapsd, tapsd], axis=1)

    parts, window, to_partner, to_beyond, mine, theirs = run_main(
        gathered,
        small,
        jnp.asarray(tap_selector(), BF16),
        taps2,
        taps2t,
        taps3,
        b_first.reshape(1, 16),
        b_middle.reshape(1, 16),
        b_last.reshape(1, 2),
    )
    partner = swapped(to_partner, size_y, lambda i: i ^ 1)
    beyond = swapped(to_beyond, size_y, lambda i: (((i + 1) ^ 1) - 1) % size_y)
    mine, (partner, beyond) = sum_over_y(mine, theirs, partner, beyond)
    field, noise_grad = run_input(partner, beyond, window, tapsd, parts, noise.reshape(2, 8, 128))
    mine, field, noise_grad = lax.optimization_barrier((mine, field, noise_grad))
    theirs = swapped(mine, size_y, lambda i: i ^ 1)
    loss, first, b1, middle, b2, last, b3 = run_unpack(1.0 / sites, mine, theirs)
    return (
        field.reshape(noise.shape),
        noise_grad.reshape(noise.shape),
        loss.reshape(()),
        jnp.transpose(first.reshape(3, 3, 3, 3, 1, 16), (5, 4, 0, 1, 2, 3)),
        b1.reshape(16),
        jnp.transpose(middle.reshape(3, 3, 3, 3, 16, 16), (4, 5, 0, 1, 2, 3)),
        b2.reshape(16),
        jnp.transpose(last.reshape(3, 3, 3, 3, 2, 16), (4, 5, 0, 1, 2, 3)),
        b3.reshape(2),
    )


def solution(mesh):
    placed = (P("gx", "gy", None, None), P(), P(), P(), P(), P(), P())
    return jax.shard_map(
        local,
        mesh=mesh,
        in_specs=placed,
        out_specs=(P("gx", "gy", None, None), P("gx", "gy", None, None)) + (P(),) * 7,
        check_vma=False,
    )
```

```python
import functools

import jax
import jax.numpy as jnp
import numpy as np
from jax import lax
from jax.experimental import pallas as pl
from jax.experimental.pallas import tpu as pltpu
from jax.sharding import PartitionSpec as P

HOPPING = 0.15
QUARTIC = 0.1
F32 = jnp.float32
BF16 = jnp.bfloat16

HALO = 6
ROWS = 2 + 2 * HALO
XP = 10
PACK_ROWS = 288
SMALL_ROWS = (112, 120)
GROUP = 8


def tap_selector():
    table = np.zeros((32, 16, 64), np.float32)
    for x in range(2):
        for y in range(2):
            for t in range(4):
                for a in range(3):
                    for b in range(3):
                        for c in range(3):
                            column = (x + a) * 16 + (y + b) * 4 + (t + c - 1) % 4
                            table[a * 9 + b * 3 + c, (x * 2 + y) * 4 + t, column] = 1.0
    return table.reshape(32, 1024)


def roll_z(v, shift):
    shift = shift % 128
    if shift == 0:
        return v
    last = v.ndim - 1
    return jnp.concatenate(
        [pltpu.roll(v[..., :128], shift, last), pltpu.roll(v[..., 128:], shift, last)], axis=last
    )


def swap_halves(v):
    return jnp.concatenate([v[..., 128:], v[..., :128]], axis=v.ndim - 1)


def iota(shape, dim):
    return lax.broadcasted_iota(jnp.int32, shape, dim)


def band_tile(taps, first, rows):
    zero = jnp.zeros((rows, 128), F32)
    left = taps[first] if 0 <= first <= 2 else zero
    right = taps[first + 1] if 0 <= first + 1 <= 2 else zero
    return jnp.where(iota((rows, 128), 1) < 64, left, right)


def build_hidden_band(taps_ref, band_ref):
    for d in range(3):
        for t in range(4):
            for a in range(3):
                taps = []
                for b in range(3):
                    tap = taps_ref[d * 9 + a * 3 + b].astype(F32)
                    taps.append(pltpu.roll(tap, (16 * (t - 1)) % 128, 1))
                for y in range(2):
                    for pair in range(2):
                        row = d * 128 + (y * 4 + t) * 16
                        lane = (a * 2 + pair) * 128
                        tile = band_tile(taps, 2 * pair - y, 16)
                        band_ref[row : row + 16, lane : lane + 128] = tile.astype(BF16)


def build_head_band(taps_ref, band_ref):
    for d in range(3):
        for x in range(2):
            for window in range(4):
                a = window - x
                for pair in range(3):
                    for half in range(2):
                        row = d * 64 + x * 32 + half * 16
                        lane = (window * 3 + pair) * 128
                        if 0 <= a <= 2:
                            taps = [taps_ref[d * 9 + a * 3 + b].astype(F32) for b in range(3)]
                            tile = jnp.concatenate(
                                [band_tile(taps, 2 * pair - 2 * half - y, 8) for y in range(2)], axis=0
                            )
                        else:
                            tile = jnp.zeros((16, 128), F32)
                        band_ref[row : row + 16, lane : lane + 128] = tile.astype(BF16)


def combine_z(parts, rows):
    return (
        roll_z(parts[:rows], 1) + parts[rows : 2 * rows] + roll_z(parts[2 * rows :], -1)
    )


def rotate_groups(v, step, lanes):
    if step == 0:
        return v
    group = (iota(v.shape, 1) // lanes) % 4
    ahead = pltpu.roll(v, (128 - lanes * step) % 128, 1)
    behind = pltpu.roll(v, lanes * (4 - step), 1)
    return jnp.where(group + step < 4, ahead, behind)


def rotate_rows(v, step):
    if step == 0:
        return v
    ahead = pltpu.roll(v, v.shape[0] - step, 0)
    behind = pltpu.roll(v, 4 - step, 0)
    return jnp.where(iota(v.shape, 0) % 4 + step < 4, ahead, behind)


def main_kernel(
    noise_ref,
    small_ref,
    selector_ref,
    taps2_ref,
    taps2t_ref,
    taps3_ref,
    b1_ref,
    b2_ref,
    b3_ref,
    parts_out,
    window_out,
    partner_out,
    beyond_out,
    mine_out,
    theirs_out,
    nz,
    inp,
    h1,
    h2,
    cm,
    cmr,
    cf,
    cl,
    head,
    phi,
    own_parts,
    w1,
    wl,
    w2,
    w2t,
    w3,
    gm,
    gl,
    gf,
    pack_out,
    raw,
    raw_sem,
):
    arriving = pltpu.make_async_copy(noise_ref, raw, raw_sem)
    arriving.start()

    def column(ref, rows, repeats):
        shape = (rows * repeats, rows)
        match = iota(shape, 0) // repeats == iota(shape, 1)
        return jnp.sum(jnp.where(match, ref[...], 0.0), axis=1, keepdims=True)

    b1 = column(b1_ref, 16, 1)
    b2 = column(b2_ref, 16, 1)
    b3 = column(b3_ref, 2, 4)

    spread = jnp.dot(small_ref[...], selector_ref[...], preferred_element_type=F32)
    for g in range(16):
        piece = spread[:, g * 64 : (g + 1) * 64]
        w1[g * 16 : (g + 1) * 16, :] = jnp.concatenate(
            [piece[16 * k : 16 * k + 16] for k in range(3)], axis=1
        ).astype(BF16)
        wl[g * 16 : (g + 1) * 16, :] = jnp.concatenate(
            [piece[48 + 16 * k : 64 + 16 * k] for k in range(6)], axis=1
        ).astype(BF16)
    build_hidden_band(taps2_ref, w2)
    build_hidden_band(taps2t_ref, w2t)
    build_head_band(taps3_ref, w3)

    arriving.wait()

    rows_in = 4 * ROWS
    shape = (rows_in, 256)
    site = iota(shape, 0) // 4 + iota(shape, 0) % 4 + iota(shape, 1) % 128
    even = site % 2
    for xl in range(8):
        v = jnp.concatenate([raw[xl], raw[xl + 8]], axis=1).astype(F32)
        nz[xl + 1] = v
        if xl == 7:
            nz[0] = swap_halves(v)
        if xl == 0:
            nz[9] = swap_halves(v)
    for xl in range(XP):
        v = jnp.where(even == (xl + 1) % 2, nz[xl], 0.0)
        inp[0, xl] = roll_z(v, 1)
        inp[1, xl] = v
        inp[2, xl] = roll_z(v, -1)

    def wrap(ref):
        ref[0] = swap_halves(ref[8])
        ref[9] = swap_halves(ref[1])

    def first_body(step, _):
        xp = step // 6
        yp = step % 6
        window = inp[:, pl.ds(2 * xp, 4), pl.ds(pl.multiple_of(8 * yp, 8), 16), :]
        window = window.reshape(192, 256).astype(BF16)
        out = jnp.dot(w1[...], window, preferred_element_type=F32)
        out = jnp.tanh(out.reshape(16, 16, 256) + b1[None]).reshape(256, 256).astype(BF16)
        row = pl.ds(pl.multiple_of(yp * 128, 128), 128)
        h1[2 * xp + 1, row, :] = out[:128]
        h1[2 * xp + 2, row, :] = out[128:]
        return 0

    lax.fori_loop(0, 24, first_body, 0, unroll=24)
    wrap(h1)

    def second_body(step, _):
        xl = step // 5
        yp = step % 5
        window = h1[pl.ds(xl, 3), pl.ds(pl.multiple_of(yp * 128, 128), 256), :].reshape(768, 256)
        parts = jnp.dot(w2[...], window, preferred_element_type=F32)
        out = combine_z(parts, 128)
        out = jnp.tanh(out.reshape(8, 16, 256) + b2[None]).reshape(128, 256)
        h2[xl + 1, pl.ds(pl.multiple_of(yp * 128, 128), 128), :] = out.astype(BF16)
        return 0

    lax.fori_loop(0, 40, second_body, 0, unroll=40)
    wrap(h2)

    top = iota((8, 256), 0) < 4

    def head_body(step, _):
        xp = step // 2
        yq = step % 2
        window = h2[pl.ds(2 * xp, 4), pl.ds(pl.multiple_of(yq * 256, 256), 384), :].reshape(1536, 256)
        parts = jnp.dot(w3[...], window, preferred_element_type=F32)
        out = combine_z(parts, 64)
        out = (out.reshape(8, 8, 256) + b3[None]).reshape(64, 256)
        for x in range(2):
            for pair in range(2):
                base = x * 32 + pair * 16
                lower = out[base : base + 8]
                upper = out[base + 8 : base + 16]
                row = pl.ds(pl.multiple_of(yq * 16, 16) + pair * 8, 8)
                head[0, 2 * xp + x, row, :] = jnp.where(top, lower, pltpu.roll(upper, 4, 0))
                head[1, 2 * xp + x, row, :] = jnp.where(top, pltpu.roll(lower, 4, 0), upper)
        return 0

    lax.fori_loop(0, 8, head_body, 0, unroll=8)

    shape = (32, 256)
    row32 = iota(shape, 0)
    site = row32 // 4 + 1 + row32 % 4 + iota(shape, 1) % 128
    even = site % 2
    for xl in range(8):
        frozen = even == xl % 2
        noise = nz[xl + 1, 12:44, :]
        log_scale = jnp.tanh(head[0, xl])
        head[0, xl] = log_scale
        moved = noise * jnp.exp(log_scale) + head[1, xl]
        phi[xl + 1] = jnp.where(frozen, noise, moved)
    wrap(phi)

    own = (row32 >= 12) & (row32 < 20)
    inner_t = row32 % 4
    loss = jnp.zeros(shape, F32)
    cot_sum = [jnp.zeros((8, 256), F32), jnp.zeros((8, 256), F32)]
    for xl in range(8):
        frozen = even == xl % 2
        noise = nz[xl + 1, 12:44, :]
        log_scale = head[0, xl]
        growth = jnp.exp(log_scale)
        here = phi[xl + 1]
        upward = (
            phi[xl + 2]
            + pltpu.roll(here, 28, 0)
            + jnp.where(inner_t == 3, pltpu.roll(here, 3, 0), pltpu.roll(here, 31, 0))
            + roll_z(here, -1)
        )
        downward = (
            phi[xl]
            + pltpu.roll(here, 4, 0)
            + jnp.where(inner_t == 0, pltpu.roll(here, 29, 0), pltpu.roll(here, 1, 0))
            + roll_z(here, 1)
        )
        squared = here * here
        density = (
            -2.0 * HOPPING * here * upward + squared + QUARTIC * (squared - 1.0) * (squared - 1.0)
        )
        local = -0.5 * noise * noise - jnp.where(frozen, 0.0, log_scale) + density
        loss = loss + jnp.where(own, local, 0.0)
        force = (
            -2.0 * HOPPING * (upward + downward)
            + 2.0 * here
            + 4.0 * QUARTIC * here * (squared - 1.0)
        )
        d_scale = (force * noise * growth - 1.0) * (1.0 - log_scale * log_scale)
        pair = (jnp.where(frozen, 0.0, d_scale), jnp.where(frozen, 0.0, force))
        own_parts[0, xl] = growth[12:20]
        own_parts[1, xl] = head[1, xl][12:20]
        own_parts[2, xl] = (upward + downward)[12:20]
        for ch in range(2):
            v = pltpu.roll(pair[ch], 28, 0)[:24].astype(BF16).astype(F32)
            cot_sum[ch] = cot_sum[ch] + v[8:16]
            for d, shift in ((0, 1), (1, 0), (2, -1)):
                moved = roll_z(v, shift)
                cl[d, ch, xl + 1] = moved
                if xl == 7:
                    cl[d, ch, 0] = swap_halves(moved)
                if xl == 0:
                    cl[d, ch, 9] = swap_halves(moved)

    def middle_body(step, _):
        xp = step // 2
        yp = step % 2
        window = cl[:, :, pl.ds(2 * xp, 4), pl.ds(pl.multiple_of(8 * yp, 8), 16), :]
        window = window.reshape(384, 256).astype(BF16)
        out = jnp.dot(wl[...], window, preferred_element_type=F32)
        for x in range(2):
            hidden = h2[2 * xp + 1 + x, pl.ds(pl.multiple_of((3 + 2 * yp) * 64, 64), 128), :].astype(F32)
            v = out[128 * x : 128 * x + 128] * (1.0 - hidden * hidden)
            cm[2 * xp + 1 + x, pl.ds(pl.multiple_of(yp * 128, 128), 128), :] = v.astype(BF16)
        return 0

    lax.fori_loop(0, 8, middle_body, 0, unroll=8)
    wrap(cm)

    def shift_body(xl, _):
        v = cm[xl, 64:192, :].astype(F32)
        cmr[0, xl] = roll_z(v, -1).astype(BF16)
        cmr[1, xl] = v.astype(BF16)
        cmr[2, xl] = roll_z(v, 1).astype(BF16)
        return 0

    lax.fori_loop(0, XP, shift_body, 0, unroll=5)

    def first_cot_body(xl, _):
        window = cm[pl.ds(xl, 3)].reshape(768, 256)
        parts = jnp.dot(w2t[...], window, preferred_element_type=F32)
        out = combine_z(parts, 128)
        hidden = h1[xl + 1, 320:448, :].astype(F32)
        cf[xl + 1] = (out * (1.0 - hidden * hidden)).astype(BF16)
        return 0

    lax.fori_loop(0, 8, first_cot_body, 0, unroll=8)
    wrap(cf)

    gm[...] = jnp.zeros_like(gm)
    gl[...] = jnp.zeros_like(gl)
    gf[...] = jnp.zeros_like(gf)
    over_lanes = (((1,), (1,)), ((), ()))

    def grad_body(step, _):
        xs = [GROUP * step + 1 + k for k in range(GROUP)]

        def along(parts):
            return jnp.concatenate(parts, axis=1)

        left = along([cmr[:, pl.ds(x - 1, 3)].reshape(1152, 256) for x in xs])
        right = along([h1[x, 256:512, :] for x in xs])
        gm[...] += lax.dot_general(left, right, over_lanes, preferred_element_type=F32)
        left = along([cl[:, :, pl.ds(x - 1, 3), 8:16, :].reshape(144, 256).astype(BF16) for x in xs])
        right = along([h2[x, 192:448, :] for x in xs])
        gl[...] += lax.dot_general(left, right, over_lanes, preferred_element_type=F32)
        left = along([inp[:, pl.ds(x - 1, 3), 20:36, :].reshape(144, 256).astype(BF16) for x in xs])
        right = along([cf[x] for x in xs])
        gf[...] += lax.dot_general(left, right, over_lanes, preferred_element_type=F32)
        return 0

    lax.fori_loop(0, 8 // GROUP, grad_body, 0)

    low = iota((16, 128), 1) < 64
    third = []
    for g in range(9):
        sums = []
        for y in range(2):
            for side in range(2):
                total = None
                for t in range(4):
                    row = g * 128 + y * 64 + t * 16
                    block = gm[row : row + 16, side * 128 : side * 128 + 128]
                    block = rotate_groups(block, (t - 1) % 4, 16)
                    total = block if total is None else total + block
                sums.append(total)
        u0, u1, v0, v1 = sums
        v0 = pltpu.roll(v0, 64, 1)
        v1 = pltpu.roll(v1, 64, 1)
        pack_out[g * 16 : g * 16 + 16, :] = u0 + jnp.where(low, v0, v1)
        third.append(u1 + v1)
    v = gf[...]
    shape = (144, 128)
    total = jnp.zeros(shape, F32)
    for y in range(2):
        for t in range(4):
            moved = v if y + t == 0 else pltpu.roll(v, 128 - (y * 64 + t * 16), 1)
            if y:
                moved = pltpu.roll(moved, 140, 0)
            total = total + rotate_rows(moved, (t - 1) % 4)
    total = jnp.where(iota(shape, 1) < 16, total, 0.0)
    packed = total[:16]
    for g in range(1, 8):
        packed = packed + pltpu.roll(total[g * 16 : g * 16 + 16], 16 * g, 1)
    pack_out[224:240, :] = packed
    third.append(total[128:144])
    for g in range(5):
        packed = jnp.where(low, third[2 * g], pltpu.roll(third[2 * g + 1], 64, 1))
        pack_out[144 + g * 16 : 160 + g * 16, :] = packed

    shape = (144, 128)
    row144 = iota(shape, 0)
    sides = []
    for side in range(2):
        v = gl[:, side * 128 : side * 128 + 128]
        total = jnp.zeros(shape, F32)
        for t in range(4):
            total = total + jnp.where(row144 % 4 == t, rotate_groups(v, (t - 1) % 4, 16), 0.0)
        sides.append(total)
    lower_y = (row144 // 4) % 2 == 0
    r0, r1 = sides
    s0 = pltpu.roll(r0, 64, 1)
    s1 = pltpu.roll(r1, 64, 1)
    low = iota(shape, 1) < 64
    both = jnp.where(lower_y, r0, jnp.where(low, s0, s1))
    last = jnp.where(lower_y, r1, s1)
    pack_out[240:288, :] = jnp.zeros((48, 128), F32)
    pack_out[240:258, :] = both.reshape(18, 8, 128).sum(axis=1)
    pack_out[264:282, :] = last.reshape(18, 8, 128).sum(axis=1)

    diagonal = iota((16, 128), 0) == iota((16, 128), 1)

    def channel_sum(read):
        acc = None
        for xl in range(1, 9):
            v = read(xl).astype(F32)
            v = v[:, :128] + v[:, 128:]
            acc = v if acc is None else acc + v
        acc = jnp.sum(acc.reshape(8, 16, 128).sum(axis=0), axis=1, keepdims=True)
        return jnp.sum(jnp.where(diagonal, acc, 0.0), axis=0, keepdims=True)

    pack_out[258:259, :] = channel_sum(lambda xl: cm[xl, 64:192, :])
    pack_out[259:260, :] = channel_sum(lambda xl: cf[xl])
    lane = iota((1, 128), 1)
    row = jnp.where(lane == 0, jnp.sum(cot_sum[0]), 0.0)
    row = jnp.where(lane == 1, jnp.sum(cot_sum[1]), row)
    pack_out[260:261, :] = jnp.where(lane == 2, jnp.sum(loss), row)
    core = lax.rem(lax.axis_index("gy"), 2)
    half = PACK_ROWS // 2
    mine_out[...] = pack_out[pl.ds(pl.multiple_of(core * half, 8), half), :]
    theirs_out[...] = pack_out[pl.ds(pl.multiple_of((1 - core) * half, 8), half), :]

    place = lax.axis_index("gx")
    start = 2 * (place % 4)
    high = place >= 4

    def pick(v):
        return jnp.where(high, v[:, 128:], v[:, :128])

    for x in range(2):
        for k in range(3):
            parts_out[k, x] = pick(own_parts[k, start + x])
    for x in range(4):
        window_out[x] = pick(cf[start + x])
        partner_out[x] = pick(cf[start + x, pl.ds(pl.multiple_of((1 - core) * 64, 64), 64), :])
        beyond_out[x] = pick(cf[start + x, pl.ds(pl.multiple_of(core * 64, 64), 64), :])


def input_kernel(
    partner_ref, beyond_ref, own_ref, taps_ref, parts_ref, noise_ref, field_ref, out_ref, band
):
    shape = (8, 128)
    upper = iota(shape, 0) < 4
    zero = jnp.zeros(shape, F32)
    for d in range(3):
        for window in range(4):
            for pair in range(2):
                tiles = []
                for x in range(2):
                    a = window - x
                    if 0 <= a <= 2:
                        taps = [taps_ref[d * 9 + a * 3 + b].astype(F32) for b in range(3)]
                        tiles.append(
                            jnp.where(
                                upper, band_tile(taps, 2 * pair, 8), band_tile(taps, 2 * pair - 1, 8)
                            )
                        )
                    else:
                        tiles.append(zero)
                lane = (window * 2 + pair) * 128
                band[d * 16 : d * 16 + 16, lane : lane + 128] = jnp.concatenate(tiles, axis=0).astype(BF16)
    low_core = lax.rem(lax.axis_index("gy"), 2) == 0
    left = jnp.where(low_core, beyond_ref[...], partner_ref[...])
    right = jnp.where(low_core, partner_ref[...], beyond_ref[...])
    window = jnp.concatenate([left, own_ref[...], right], axis=1).reshape(1024, 128)
    parts = jnp.dot(band[...], window, preferred_element_type=F32)
    out = pltpu.roll(parts[:16], 1, 1) + parts[16:32] + pltpu.roll(parts[32:], 127, 1)
    site = iota(shape, 0) // 4 + iota(shape, 0) % 4 + iota(shape, 1)
    for x in range(2):
        frozen = (site + x) % 2 == 0
        noise = noise_ref[x]
        growth = parts_ref[0, x]
        here = jnp.where(frozen, noise, noise * growth + parts_ref[1, x])
        force = (
            -2.0 * HOPPING * parts_ref[2, x]
            + 2.0 * here
            + 4.0 * QUARTIC * here * (here * here - 1.0)
        )
        field_ref[x] = here
        out_ref[x] = jnp.where(frozen, out[8 * x : 8 * x + 8] + force, force * growth) - noise


def vmem():
    return pl.BlockSpec(memory_space=pltpu.VMEM)


def run_main(noise, small, selector, taps2, taps2t, taps3, b1, b2, b3):
    scratch = [
        ((XP, 4 * ROWS, 256), F32),
        ((3, XP, 4 * ROWS, 256), F32),
        ((XP, 768, 256), BF16),
        ((XP, 640, 256), BF16),
        ((XP, 256, 256), BF16),
        ((3, XP, 128, 256), BF16),
        ((XP, 128, 256), BF16),
        ((3, 2, XP, 24, 256), F32),
        ((2, 8, 32, 256), F32),
        ((XP, 32, 256), F32),
        ((3, 8, 8, 256), F32),
        ((256, 192), BF16),
        ((256, 384), BF16),
        ((384, 768), BF16),
        ((384, 768), BF16),
        ((192, 1536), BF16),
        ((1152, 256), F32),
        ((144, 256), F32),
        ((144, 128), F32),
        ((PACK_ROWS, 128), F32),
        ((16, 4 * ROWS, 128), BF16),
    ]
    return pl.pallas_call(
        main_kernel,
        out_shape=(
            jax.ShapeDtypeStruct((3, 2, 8, 128), F32),
            jax.ShapeDtypeStruct((4, 128, 128), BF16),
            jax.ShapeDtypeStruct((4, 64, 128), BF16),
            jax.ShapeDtypeStruct((4, 64, 128), BF16),
            jax.ShapeDtypeStruct((PACK_ROWS // 2, 128), F32),
            jax.ShapeDtypeStruct((PACK_ROWS // 2, 128), F32),
        ),
        in_specs=[pl.BlockSpec(memory_space=pltpu.HBM)] + [vmem()] * 8,
        out_specs=(vmem(),) * 6,
        scratch_shapes=[pltpu.VMEM(s, t) for s, t in scratch] + [pltpu.SemaphoreType.DMA],
        compiler_params=pltpu.CompilerParams(vmem_limit_bytes=56 * 1024 * 1024),
    )(noise, small, selector, taps2, taps2t, taps3, b1, b2, b3)


def window_kernel(copies, distant_ref, block_ref, paired_ref, across_ref, out_ref):
    me = lax.axis_index("gy")
    even = lax.rem(me, 2) == 0
    even_chip = lax.rem(me // 2, 2) == 0
    for x in range(2):
        before = jnp.where(even_chip, across_ref[x], paired_ref[x])
        after = jnp.where(even_chip, paired_ref[x], across_ref[x])
        tiles = [before[:8], before[8:], block_ref[x, :8], block_ref[x, 8:], after[:8], after[8:]]
        distant = distant_ref[x]
        rows = [jnp.where(even, distant, tiles[0])]
        rows += [jnp.where(even, tiles[k - 1], tiles[k]) for k in range(1, 6)]
        rows += [jnp.where(even, tiles[5], distant)]
        window = jnp.concatenate(rows, axis=0).astype(BF16)
        for k in range(copies):
            out_ref[k, x] = window


def run_window(distant, block, paired, across):
    copies = lax.axis_size("gx")
    return pl.pallas_call(
        functools.partial(window_kernel, copies),
        out_shape=jax.ShapeDtypeStruct((copies, 2, 4 * ROWS, 128), BF16),
        in_specs=[vmem()] * 4,
        out_specs=vmem(),
        compiler_params=pltpu.CompilerParams(vmem_limit_bytes=16 * 1024 * 1024),
    )(distant, block, paired, across)


def run_input(partner, beyond, own, taps, parts, noise):
    return pl.pallas_call(
        input_kernel,
        out_shape=(jax.ShapeDtypeStruct((2, 8, 128), F32),) * 2,
        in_specs=[vmem()] * 6,
        out_specs=(vmem(),) * 2,
        scratch_shapes=[pltpu.VMEM((48, 1024), BF16)],
        compiler_params=pltpu.CompilerParams(vmem_limit_bytes=16 * 1024 * 1024),
    )(partner, beyond, own, taps, parts, noise)


def unpack_kernel(scale, mine_ref, theirs_ref, loss, first, b1, middle, b2, last, b3, both):
    core = lax.rem(lax.axis_index("gy"), 2)
    half = PACK_ROWS // 2
    both[pl.ds(pl.multiple_of(core * half, 8), half), :] = mine_ref[...] * scale
    both[pl.ds(pl.multiple_of((1 - core) * half, 8), half), :] = theirs_ref[...] * scale

    def lanes_from(v, start):
        return v if start == 0 else pltpu.roll(v, 128 - start, 1)

    for d in range(3):
        for j in range(3):
            a = 2 - j
            g = d * 3 + j
            most = both[g * 16 : g * 16 + 16, :]
            third = both[144 + (g // 2) * 16 : 160 + (g // 2) * 16, :]
            for b in range(3):
                for c in range(3):
                    if b < 2:
                        v = lanes_from(most, b * 64 + c * 16)
                    else:
                        v = lanes_from(third, (g % 2) * 64 + c * 16)
                    middle[a * 27 + b * 9 + c * 3 + d] = v[:, :16]
    for d in range(3):
        for a in range(3):
            g = d * 3 + a
            if g < 8:
                v = lanes_from(both[224:240, :], 16 * g)
            else:
                v = lanes_from(both[208:224, :], 64)
            for b in range(3):
                for c in range(3):
                    row = b * 4 + c
                    first[a * 27 + b * 9 + c * 3 + d] = v[row : row + 1, :16]
    for b in range(3):
        for c in range(3):
            if b < 2:
                v = lanes_from(both[240:264, :], b * 64 + c * 16)
            else:
                v = lanes_from(both[264:288, :], c * 16)
            for d in range(3):
                for ch in range(2):
                    for a in range(3):
                        row = (2 - d) * 6 + ch * 3 + 2 - a
                        last[a * 27 + b * 9 + c * 3 + d, ch : ch + 1, :] = v[row : row + 1, :16]
    b2[...] = both[258:259, :16]
    b1[...] = both[259:260, :16]
    row = both[260:261, :]
    b3[...] = row[:, :2]
    loss[...] = pltpu.roll(row, 126, 1)[:, :1]


def run_unpack(scale, mine, theirs):
    shapes = ((1, 1), (81, 1, 16), (1, 16), (81, 16, 16), (1, 16), (81, 2, 16), (1, 2))
    return pl.pallas_call(
        functools.partial(unpack_kernel, scale),
        out_shape=tuple(jax.ShapeDtypeStruct(s, F32) for s in shapes),
        in_specs=[vmem(), vmem()],
        out_specs=(vmem(),) * len(shapes),
        scratch_shapes=[pltpu.VMEM((PACK_ROWS, 128), F32)],
        compiler_params=pltpu.CompilerParams(vmem_limit_bytes=16 * 1024 * 1024),
    )(mine, theirs)


def pad_taps(v):
    return jnp.pad(v, [(0, 0)] * (v.ndim - 2) + [(0, 1), (0, 0)])


def taps_kernel(kernel_ref, taps_ref, flipped_ref, spread):
    shape = (16, 128)
    lane = iota(shape, 1)
    group = (lane // 16) % 4
    repeat = jnp.where(iota(shape, 0) == lane % 16, 1.0, 0.0).astype(BF16)
    spread[...] = jnp.dot(kernel_ref[...], repeat, preferred_element_type=F32)
    unit = jnp.where(iota((16, 16), 0) == iota((16, 16), 1), 1.0, 0.0).astype(BF16)
    starts = [128 * k for k in range(10)] + [1168]
    turned = [
        lax.dot_general(
            unit, kernel_ref[k : k + 128, :], (((1,), (1,)), ((), ())), preferred_element_type=F32
        )
        for k in starts
    ]
    zero = jnp.zeros(shape, F32)
    for d in range(3):
        for a in range(3):
            for b in range(3):
                plain = zero
                flipped = zero
                for c in range(3):
                    tap = a * 27 + b * 9 + c * 3 + d
                    plain = jnp.where(group == c, spread[tap * 16 : tap * 16 + 16, :], plain)
                    tap = 80 - tap
                    chunk = tap // 8
                    offset = tap * 16 - starts[chunk]
                    shift = (c * 16 - offset) % 128
                    v = turned[chunk]
                    v = pltpu.roll(v, shift, 1) if shift else v
                    flipped = jnp.where(lane // 16 == c, v, flipped)
                flipped = flipped + pltpu.roll(flipped, 64, 1)
                taps_ref[d * 9 + a * 3 + b] = plain.astype(BF16)
                flipped_ref[d * 9 + a * 3 + b] = flipped.astype(BF16)


def hidden_taps(kernel):
    return pl.pallas_call(
        taps_kernel,
        out_shape=(jax.ShapeDtypeStruct((27, 16, 128), BF16),) * 2,
        in_specs=[vmem()],
        out_specs=(vmem(),) * 2,
        scratch_shapes=[pltpu.VMEM((1296, 128), F32)],
        compiler_params=pltpu.CompilerParams(vmem_limit_bytes=16 * 1024 * 1024),
    )(jnp.transpose(kernel, (2, 3, 4, 5, 0, 1)).reshape(1296, 16))


def banded_taps(v):
    v = pad_taps(v)
    v = jnp.stack([jnp.roll(v, t - 1, axis=2) for t in range(4)], axis=2)
    v = v.reshape(27, -1, 64)
    return jnp.concatenate([v, v], axis=2)


def swapped(v, axis_size, partner):
    return lax.ppermute(v, "gy", [(i, partner(i)) for i in range(axis_size)])


def gather_y(noise, weights):
    size_y = lax.axis_size("gy")
    even = lax.axis_index("gy") % 2 == 0
    chips = size_y // 2

    def far(i):
        return (i - 3) % size_y if i % 2 == 0 else (i + 3) % size_y

    def chip_after(i):
        return ((((i >> 1) + 1) ^ 1) - 1) % chips * 2 + (i & 1)

    distant = swapped(noise, size_y, far)
    beside = swapped(noise, size_y, lambda i: i ^ 1)
    block = jnp.concatenate(
        [jnp.where(even, noise, beside), jnp.where(even, beside, noise)], axis=1
    )
    block, *weights = lax.optimization_barrier((block, *weights))
    paired = swapped(block, size_y, lambda i: i ^ 2)
    across = swapped(block, size_y, chip_after)
    return run_window(
        distant.reshape(2, 8, 128),
        block.reshape(2, 16, 128),
        paired.reshape(2, 16, 128),
        across.reshape(2, 16, 128),
    ), weights


def add_rounded(v, partner):
    size_y = lax.axis_size("gy")
    first, last = SMALL_ROWS
    high = lax.reduce_precision(v, 8, 7)
    low = lax.reduce_precision(v[first:last] - high[first:last], 8, 7)
    got = swapped(jnp.concatenate([high, low], axis=0).astype(BF16), size_y, partner).astype(F32)
    rows = v.shape[0]
    total = high + got[:rows]
    small = total[first:last] + (low + got[rows:])
    return jnp.concatenate([total[:first], small, total[last:]], axis=0)


def sum_over_y(mine, theirs, *before_last):
    size_y = lax.axis_size("gy")

    def along_z(partner):
        def f(i):
            return ((i >> 4) * 8 + partner((i >> 1) & 7)) * 2 + (i & 1)

        return f

    crossing = (3, 6, 5, 0, 7, 2, 1, 4)
    v = mine + swapped(theirs, size_y, lambda i: i ^ 1)
    v = add_rounded(v, lambda i: i ^ 16)
    v = add_rounded(v, along_z(lambda z: z ^ 1))
    v, *before_last = lax.optimization_barrier((v, *before_last))
    v = add_rounded(v, along_z(lambda z: (((z + 1) ^ 1) - 1) % 8))
    v = add_rounded(v, along_z(lambda z: crossing[z]))
    return v, before_last


def local(noise, w_first, b_first, w_middle, b_middle, w_last, b_last):
    size_y = lax.axis_size("gy")
    sites = float(noise.size * lax.axis_size("gx") * size_y)
    sent, (w_first, w_middle, w_last) = gather_y(noise, (w_first, w_middle, w_last))
    gathered = lax.all_to_all(sent, "gx", 0, 0, tiled=True).reshape(16, 4 * ROWS, 128)
    flip = (slice(None), slice(None)) + (slice(None, None, -1),) * 4
    small = jnp.concatenate(
        [
            jnp.transpose(w_first[:, 0], (4, 0, 1, 2, 3)).reshape(48, 27),
            jnp.transpose(w_last[flip], (5, 0, 1, 2, 3, 4)).reshape(96, 27),
        ],
        axis=0,
    )
    small = jnp.pad(small, ((0, 0), (0, 5)))
    taps2, taps2t = hidden_taps(w_middle)
    taps3 = banded_taps(jnp.transpose(w_last, (5, 2, 3, 0, 4, 1)).reshape(27, 2, 3, 16))
    tapsd = banded_taps(jnp.transpose(w_first[flip], (5, 2, 3, 1, 4, 0)).reshape(27, 1, 3, 16))
    tapsd = jnp.concatenate([tapsd, tapsd], axis=1)

    parts, window, to_partner, to_beyond, mine, theirs = run_main(
        gathered,
        small,
        jnp.asarray(tap_selector(), BF16),
        taps2,
        taps2t,
        taps3,
        b_first.reshape(1, 16),
        b_middle.reshape(1, 16),
        b_last.reshape(1, 2),
    )
    partner = swapped(to_partner, size_y, lambda i: i ^ 1)
    beyond = swapped(to_beyond, size_y, lambda i: (((i + 1) ^ 1) - 1) % size_y)
    mine, (partner, beyond) = sum_over_y(mine, theirs, partner, beyond)
    field, noise_grad = run_input(partner, beyond, window, tapsd, parts, noise.reshape(2, 8, 128))
    mine, field, noise_grad = lax.optimization_barrier((mine, field, noise_grad))
    theirs = swapped(mine, size_y, lambda i: i ^ 1)
    loss, first, b1, middle, b2, last, b3 = run_unpack(1.0 / sites, mine, theirs)
    return (
        field.reshape(noise.shape),
        noise_grad.reshape(noise.shape),
        loss.reshape(()),
        jnp.transpose(first.reshape(3, 3, 3, 3, 1, 16), (5, 4, 0, 1, 2, 3)),
        b1.reshape(16),
        jnp.transpose(middle.reshape(3, 3, 3, 3, 16, 16), (4, 5, 0, 1, 2, 3)),
        b2.reshape(16),
        jnp.transpose(last.reshape(3, 3, 3, 3, 2, 16), (4, 5, 0, 1, 2, 3)),
        b3.reshape(2),
    )


def solution(mesh):
    placed = (P("gx", "gy", None, None), P(), P(), P(), P(), P(), P())
    return jax.shard_map(
        local,
        mesh=mesh,
        in_specs=placed,
        out_specs=(P("gx", "gy", None, None), P("gx", "gy", None, None)) + (P(),) * 7,
        check_vma=False,
    )
```

```python
import functools

import jax
import jax.numpy as jnp
import numpy as np
from jax import lax
from jax.experimental import pallas as pl
from jax.experimental.pallas import tpu as pltpu
from jax.sharding import PartitionSpec as P

HOPPING = 0.15
QUARTIC = 0.1
F32 = jnp.float32
BF16 = jnp.bfloat16

HALO = 6
ROWS = 2 + 2 * HALO
XP = 10
PACK_ROWS = 288
GROUP = 8


def tap_selector():
    table = np.zeros((32, 16, 64), np.float32)
    for x in range(2):
        for y in range(2):
            for t in range(4):
                for a in range(3):
                    for b in range(3):
                        for c in range(3):
                            column = (x + a) * 16 + (y + b) * 4 + (t + c - 1) % 4
                            table[a * 9 + b * 3 + c, (x * 2 + y) * 4 + t, column] = 1.0
    return table.reshape(32, 1024)


def roll_z(v, shift):
    shift = shift % 128
    if shift == 0:
        return v
    last = v.ndim - 1
    return jnp.concatenate(
        [pltpu.roll(v[..., :128], shift, last), pltpu.roll(v[..., 128:], shift, last)], axis=last
    )


def swap_halves(v):
    return jnp.concatenate([v[..., 128:], v[..., :128]], axis=v.ndim - 1)


def iota(shape, dim):
    return lax.broadcasted_iota(jnp.int32, shape, dim)


def band_tile(taps, first, rows):
    zero = jnp.zeros((rows, 128), F32)
    left = taps[first] if 0 <= first <= 2 else zero
    right = taps[first + 1] if 0 <= first + 1 <= 2 else zero
    return jnp.where(iota((rows, 128), 1) < 64, left, right)


def build_hidden_band(taps_ref, band_ref):
    for d in range(3):
        for t in range(4):
            for a in range(3):
                taps = []
                for b in range(3):
                    tap = taps_ref[d * 9 + a * 3 + b].astype(F32)
                    taps.append(pltpu.roll(tap, (16 * (t - 1)) % 128, 1))
                for y in range(2):
                    for pair in range(2):
                        row = d * 128 + (y * 4 + t) * 16
                        lane = (a * 2 + pair) * 128
                        tile = band_tile(taps, 2 * pair - y, 16)
                        band_ref[row : row + 16, lane : lane + 128] = tile.astype(BF16)


def build_head_band(taps_ref, band_ref):
    for d in range(3):
        for x in range(2):
            for window in range(4):
                a = window - x
                for pair in range(3):
                    for half in range(2):
                        row = d * 64 + x * 32 + half * 16
                        lane = (window * 3 + pair) * 128
                        if 0 <= a <= 2:
                            taps = [taps_ref[d * 9 + a * 3 + b].astype(F32) for b in range(3)]
                            tile = jnp.concatenate(
                                [band_tile(taps, 2 * pair - 2 * half - y, 8) for y in range(2)], axis=0
                            )
                        else:
                            tile = jnp.zeros((16, 128), F32)
                        band_ref[row : row + 16, lane : lane + 128] = tile.astype(BF16)


def combine_z(parts, rows):
    return (
        roll_z(parts[:rows], 1) + parts[rows : 2 * rows] + roll_z(parts[2 * rows :], -1)
    )


def rotate_groups(v, step, lanes):
    if step == 0:
        return v
    group = (iota(v.shape, 1) // lanes) % 4
    ahead = pltpu.roll(v, (128 - lanes * step) % 128, 1)
    behind = pltpu.roll(v, lanes * (4 - step), 1)
    return jnp.where(group + step < 4, ahead, behind)


def rotate_rows(v, step):
    if step == 0:
        return v
    ahead = pltpu.roll(v, v.shape[0] - step, 0)
    behind = pltpu.roll(v, 4 - step, 0)
    return jnp.where(iota(v.shape, 0) % 4 + step < 4, ahead, behind)


def main_kernel(
    noise_ref,
    small_ref,
    selector_ref,
    taps2_ref,
    taps2t_ref,
    taps3_ref,
    b1_ref,
    b2_ref,
    b3_ref,
    parts_out,
    window_out,
    partner_out,
    beyond_out,
    mine_out,
    theirs_out,
    nz,
    inp,
    h1,
    h2,
    cm,
    cmr,
    cf,
    cl,
    head,
    phi,
    own_parts,
    w1,
    wl,
    w2,
    w2t,
    w3,
    gm,
    gl,
    gf,
    pack_out,
    raw,
    raw_sem,
):
    arriving = pltpu.make_async_copy(noise_ref, raw, raw_sem)
    arriving.start()

    def column(ref, rows, repeats):
        shape = (rows * repeats, rows)
        match = iota(shape, 0) // repeats == iota(shape, 1)
        return jnp.sum(jnp.where(match, ref[...], 0.0), axis=1, keepdims=True)

    b1 = column(b1_ref, 16, 1)
    b2 = column(b2_ref, 16, 1)
    b3 = column(b3_ref, 2, 4)

    spread = jnp.dot(small_ref[...], selector_ref[...], preferred_element_type=F32)
    for g in range(16):
        piece = spread[:, g * 64 : (g + 1) * 64]
        w1[g * 16 : (g + 1) * 16, :] = jnp.concatenate(
            [piece[16 * k : 16 * k + 16] for k in range(3)], axis=1
        ).astype(BF16)
        wl[g * 16 : (g + 1) * 16, :] = jnp.concatenate(
            [piece[48 + 16 * k : 64 + 16 * k] for k in range(6)], axis=1
        ).astype(BF16)
    build_hidden_band(taps2_ref, w2)
    build_hidden_band(taps2t_ref, w2t)
    build_head_band(taps3_ref, w3)

    arriving.wait()

    rows_in = 4 * ROWS
    shape = (rows_in, 256)
    site = iota(shape, 0) // 4 + iota(shape, 0) % 4 + iota(shape, 1) % 128
    even = site % 2
    for xl in range(8):
        v = jnp.concatenate([raw[xl], raw[xl + 8]], axis=1).astype(F32)
        nz[xl + 1] = v
        if xl == 7:
            nz[0] = swap_halves(v)
        if xl == 0:
            nz[9] = swap_halves(v)
    for xl in range(XP):
        v = jnp.where(even == (xl + 1) % 2, nz[xl], 0.0)
        inp[0, xl] = roll_z(v, 1)
        inp[1, xl] = v
        inp[2, xl] = roll_z(v, -1)

    def wrap(ref):
        ref[0] = swap_halves(ref[8])
        ref[9] = swap_halves(ref[1])

    def first_body(step, _):
        xp = step // 6
        yp = step % 6
        window = inp[:, pl.ds(2 * xp, 4), pl.ds(pl.multiple_of(8 * yp, 8), 16), :]
        window = window.reshape(192, 256).astype(BF16)
        out = jnp.dot(w1[...], window, preferred_element_type=F32)
        out = jnp.tanh(out.reshape(16, 16, 256) + b1[None]).reshape(256, 256).astype(BF16)
        row = pl.ds(pl.multiple_of(yp * 128, 128), 128)
        h1[2 * xp + 1, row, :] = out[:128]
        h1[2 * xp + 2, row, :] = out[128:]
        return 0

    lax.fori_loop(0, 24, first_body, 0, unroll=24)
    wrap(h1)

    def second_body(step, _):
        xl = step // 5
        yp = step % 5
        window = h1[pl.ds(xl, 3), pl.ds(pl.multiple_of(yp * 128, 128), 256), :].reshape(768, 256)
        parts = jnp.dot(w2[...], window, preferred_element_type=F32)
        out = combine_z(parts, 128)
        out = jnp.tanh(out.reshape(8, 16, 256) + b2[None]).reshape(128, 256)
        h2[xl + 1, pl.ds(pl.multiple_of(yp * 128, 128), 128), :] = out.astype(BF16)
        return 0

    lax.fori_loop(0, 40, second_body, 0, unroll=40)
    wrap(h2)

    top = iota((8, 256), 0) < 4

    def head_body(step, _):
        xp = step // 2
        yq = step % 2
        window = h2[pl.ds(2 * xp, 4), pl.ds(pl.multiple_of(yq * 256, 256), 384), :].reshape(1536, 256)
        parts = jnp.dot(w3[...], window, preferred_element_type=F32)
        out = combine_z(parts, 64)
        out = (out.reshape(8, 8, 256) + b3[None]).reshape(64, 256)
        for x in range(2):
            for pair in range(2):
                base = x * 32 + pair * 16
                lower = out[base : base + 8]
                upper = out[base + 8 : base + 16]
                row = pl.ds(pl.multiple_of(yq * 16, 16) + pair * 8, 8)
                head[0, 2 * xp + x, row, :] = jnp.where(top, lower, pltpu.roll(upper, 4, 0))
                head[1, 2 * xp + x, row, :] = jnp.where(top, pltpu.roll(lower, 4, 0), upper)
        return 0

    lax.fori_loop(0, 8, head_body, 0, unroll=8)

    shape = (32, 256)
    row32 = iota(shape, 0)
    site = row32 // 4 + 1 + row32 % 4 + iota(shape, 1) % 128
    even = site % 2
    for xl in range(8):
        frozen = even == xl % 2
        noise = nz[xl + 1, 12:44, :]
        log_scale = jnp.tanh(head[0, xl])
        head[0, xl] = log_scale
        moved = noise * jnp.exp(log_scale) + head[1, xl]
        phi[xl + 1] = jnp.where(frozen, noise, moved)
    wrap(phi)

    own = (row32 >= 12) & (row32 < 20)
    inner_t = row32 % 4
    loss = jnp.zeros(shape, F32)
    cot_sum = [jnp.zeros((8, 256), F32), jnp.zeros((8, 256), F32)]
    for xl in range(8):
        frozen = even == xl % 2
        noise = nz[xl + 1, 12:44, :]
        log_scale = head[0, xl]
        growth = jnp.exp(log_scale)
        here = phi[xl + 1]
        upward = (
            phi[xl + 2]
            + pltpu.roll(here, 28, 0)
            + jnp.where(inner_t == 3, pltpu.roll(here, 3, 0), pltpu.roll(here, 31, 0))
            + roll_z(here, -1)
        )
        downward = (
            phi[xl]
            + pltpu.roll(here, 4, 0)
            + jnp.where(inner_t == 0, pltpu.roll(here, 29, 0), pltpu.roll(here, 1, 0))
            + roll_z(here, 1)
        )
        squared = here * here
        density = (
            -2.0 * HOPPING * here * upward + squared + QUARTIC * (squared - 1.0) * (squared - 1.0)
        )
        local = -0.5 * noise * noise - jnp.where(frozen, 0.0, log_scale) + density
        loss = loss + jnp.where(own, local, 0.0)
        force = (
            -2.0 * HOPPING * (upward + downward)
            + 2.0 * here
            + 4.0 * QUARTIC * here * (squared - 1.0)
        )
        d_scale = (force * noise * growth - 1.0) * (1.0 - log_scale * log_scale)
        pair = (jnp.where(frozen, 0.0, d_scale), jnp.where(frozen, 0.0, force))
        own_parts[0, xl] = growth[12:20]
        own_parts[1, xl] = head[1, xl][12:20]
        own_parts[2, xl] = (upward + downward)[12:20]
        for ch in range(2):
            v = pltpu.roll(pair[ch], 28, 0)[:24].astype(BF16).astype(F32)
            cot_sum[ch] = cot_sum[ch] + v[8:16]
            for d, shift in ((0, 1), (1, 0), (2, -1)):
                moved = roll_z(v, shift)
                cl[d, ch, xl + 1] = moved
                if xl == 7:
                    cl[d, ch, 0] = swap_halves(moved)
                if xl == 0:
                    cl[d, ch, 9] = swap_halves(moved)

    def middle_body(step, _):
        xp = step // 2
        yp = step % 2
        window = cl[:, :, pl.ds(2 * xp, 4), pl.ds(pl.multiple_of(8 * yp, 8), 16), :]
        window = window.reshape(384, 256).astype(BF16)
        out = jnp.dot(wl[...], window, preferred_element_type=F32)
        for x in range(2):
            hidden = h2[2 * xp + 1 + x, pl.ds(pl.multiple_of((3 + 2 * yp) * 64, 64), 128), :].astype(F32)
            v = out[128 * x : 128 * x + 128] * (1.0 - hidden * hidden)
            cm[2 * xp + 1 + x, pl.ds(pl.multiple_of(yp * 128, 128), 128), :] = v.astype(BF16)
        return 0

    lax.fori_loop(0, 8, middle_body, 0, unroll=8)
    wrap(cm)

    def shift_body(xl, _):
        v = cm[xl, 64:192, :].astype(F32)
        cmr[0, xl] = roll_z(v, -1).astype(BF16)
        cmr[1, xl] = v.astype(BF16)
        cmr[2, xl] = roll_z(v, 1).astype(BF16)
        return 0

    lax.fori_loop(0, XP, shift_body, 0, unroll=5)

    def first_cot_body(xl, _):
        window = cm[pl.ds(xl, 3)].reshape(768, 256)
        parts = jnp.dot(w2t[...], window, preferred_element_type=F32)
        out = combine_z(parts, 128)
        hidden = h1[xl + 1, 320:448, :].astype(F32)
        cf[xl + 1] = (out * (1.0 - hidden * hidden)).astype(BF16)
        return 0

    lax.fori_loop(0, 8, first_cot_body, 0, unroll=8)
    wrap(cf)

    gm[...] = jnp.zeros_like(gm)
    gl[...] = jnp.zeros_like(gl)
    gf[...] = jnp.zeros_like(gf)
    over_lanes = (((1,), (1,)), ((), ()))

    def grad_body(step, _):
        xs = [GROUP * step + 1 + k for k in range(GROUP)]

        def along(parts):
            return jnp.concatenate(parts, axis=1)

        left = along([cmr[:, pl.ds(x - 1, 3)].reshape(1152, 256) for x in xs])
        right = along([h1[x, 256:512, :] for x in xs])
        gm[...] += lax.dot_general(left, right, over_lanes, preferred_element_type=F32)
        left = along([cl[:, :, pl.ds(x - 1, 3), 8:16, :].reshape(144, 256).astype(BF16) for x in xs])
        right = along([h2[x, 192:448, :] for x in xs])
        gl[...] += lax.dot_general(left, right, over_lanes, preferred_element_type=F32)
        left = along([inp[:, pl.ds(x - 1, 3), 20:36, :].reshape(144, 256).astype(BF16) for x in xs])
        right = along([cf[x] for x in xs])
        gf[...] += lax.dot_general(left, right, over_lanes, preferred_element_type=F32)
        return 0

    lax.fori_loop(0, 8 // GROUP, grad_body, 0)

    low = iota((16, 128), 1) < 64
    third = []
    for g in range(9):
        sums = []
        for y in range(2):
            for side in range(2):
                total = None
                for t in range(4):
                    row = g * 128 + y * 64 + t * 16
                    block = gm[row : row + 16, side * 128 : side * 128 + 128]
                    block = rotate_groups(block, (t - 1) % 4, 16)
                    total = block if total is None else total + block
                sums.append(total)
        u0, u1, v0, v1 = sums
        v0 = pltpu.roll(v0, 64, 1)
        v1 = pltpu.roll(v1, 64, 1)
        pack_out[g * 16 : g * 16 + 16, :] = u0 + jnp.where(low, v0, v1)
        third.append(u1 + v1)
    v = gf[...]
    shape = (144, 128)
    total = jnp.zeros(shape, F32)
    for y in range(2):
        for t in range(4):
            moved = v if y + t == 0 else pltpu.roll(v, 128 - (y * 64 + t * 16), 1)
            if y:
                moved = pltpu.roll(moved, 140, 0)
            total = total + rotate_rows(moved, (t - 1) % 4)
    total = jnp.where(iota(shape, 1) < 16, total, 0.0)
    packed = total[:16]
    for g in range(1, 8):
        packed = packed + pltpu.roll(total[g * 16 : g * 16 + 16], 16 * g, 1)
    pack_out[224:240, :] = packed
    third.append(total[128:144])
    for g in range(5):
        packed = jnp.where(low, third[2 * g], pltpu.roll(third[2 * g + 1], 64, 1))
        pack_out[144 + g * 16 : 160 + g * 16, :] = packed

    shape = (144, 128)
    row144 = iota(shape, 0)
    sides = []
    for side in range(2):
        v = gl[:, side * 128 : side * 128 + 128]
        total = jnp.zeros(shape, F32)
        for t in range(4):
            total = total + jnp.where(row144 % 4 == t, rotate_groups(v, (t - 1) % 4, 16), 0.0)
        sides.append(total)
    lower_y = (row144 // 4) % 2 == 0
    r0, r1 = sides
    s0 = pltpu.roll(r0, 64, 1)
    s1 = pltpu.roll(r1, 64, 1)
    low = iota(shape, 1) < 64
    both = jnp.where(lower_y, r0, jnp.where(low, s0, s1))
    last = jnp.where(lower_y, r1, s1)
    pack_out[240:288, :] = jnp.zeros((48, 128), F32)
    pack_out[240:258, :] = both.reshape(18, 8, 128).sum(axis=1)
    pack_out[264:282, :] = last.reshape(18, 8, 128).sum(axis=1)

    diagonal = iota((16, 128), 0) == iota((16, 128), 1)

    def channel_sum(read):
        acc = None
        for xl in range(1, 9):
            v = read(xl).astype(F32)
            v = v[:, :128] + v[:, 128:]
            acc = v if acc is None else acc + v
        acc = jnp.sum(acc.reshape(8, 16, 128).sum(axis=0), axis=1, keepdims=True)
        return jnp.sum(jnp.where(diagonal, acc, 0.0), axis=0, keepdims=True)

    pack_out[258:259, :] = channel_sum(lambda xl: cm[xl, 64:192, :])
    pack_out[259:260, :] = channel_sum(lambda xl: cf[xl])
    lane = iota((1, 128), 1)
    row = jnp.where(lane == 0, jnp.sum(cot_sum[0]), 0.0)
    row = jnp.where(lane == 1, jnp.sum(cot_sum[1]), row)
    pack_out[260:261, :] = jnp.where(lane == 2, jnp.sum(loss), row)
    core = lax.rem(lax.axis_index("gy"), 2)
    half = PACK_ROWS // 2
    mine_out[...] = pack_out[pl.ds(pl.multiple_of(core * half, 8), half), :]
    theirs_out[...] = pack_out[pl.ds(pl.multiple_of((1 - core) * half, 8), half), :]

    place = lax.axis_index("gx")
    start = 2 * (place % 4)
    high = place >= 4

    def pick(v):
        return jnp.where(high, v[:, 128:], v[:, :128])

    for x in range(2):
        for k in range(3):
            parts_out[k, x] = pick(own_parts[k, start + x])
    for x in range(4):
        window_out[x] = pick(cf[start + x])
        partner_out[x] = pick(cf[start + x, pl.ds(pl.multiple_of((1 - core) * 64, 64), 64), :])
        beyond_out[x] = pick(cf[start + x, pl.ds(pl.multiple_of(core * 64, 64), 64), :])


def input_kernel(
    partner_ref, beyond_ref, own_ref, taps_ref, parts_ref, noise_ref, field_ref, out_ref, band
):
    shape = (8, 128)
    upper = iota(shape, 0) < 4
    zero = jnp.zeros(shape, F32)
    for d in range(3):
        for window in range(4):
            for pair in range(2):
                tiles = []
                for x in range(2):
                    a = window - x
                    if 0 <= a <= 2:
                        taps = [taps_ref[d * 9 + a * 3 + b].astype(F32) for b in range(3)]
                        tiles.append(
                            jnp.where(
                                upper, band_tile(taps, 2 * pair, 8), band_tile(taps, 2 * pair - 1, 8)
                            )
                        )
                    else:
                        tiles.append(zero)
                lane = (window * 2 + pair) * 128
                band[d * 16 : d * 16 + 16, lane : lane + 128] = jnp.concatenate(tiles, axis=0).astype(BF16)
    low_core = lax.rem(lax.axis_index("gy"), 2) == 0
    left = jnp.where(low_core, beyond_ref[...], partner_ref[...])
    right = jnp.where(low_core, partner_ref[...], beyond_ref[...])
    window = jnp.concatenate([left, own_ref[...], right], axis=1).reshape(1024, 128)
    parts = jnp.dot(band[...], window, preferred_element_type=F32)
    out = pltpu.roll(parts[:16], 1, 1) + parts[16:32] + pltpu.roll(parts[32:], 127, 1)
    site = iota(shape, 0) // 4 + iota(shape, 0) % 4 + iota(shape, 1)
    for x in range(2):
        frozen = (site + x) % 2 == 0
        noise = noise_ref[x]
        growth = parts_ref[0, x]
        here = jnp.where(frozen, noise, noise * growth + parts_ref[1, x])
        force = (
            -2.0 * HOPPING * parts_ref[2, x]
            + 2.0 * here
            + 4.0 * QUARTIC * here * (here * here - 1.0)
        )
        field_ref[x] = here
        out_ref[x] = jnp.where(frozen, out[8 * x : 8 * x + 8] + force, force * growth) - noise


def vmem():
    return pl.BlockSpec(memory_space=pltpu.VMEM)


def run_main(noise, small, selector, taps2, taps2t, taps3, b1, b2, b3):
    scratch = [
        ((XP, 4 * ROWS, 256), F32),
        ((3, XP, 4 * ROWS, 256), F32),
        ((XP, 768, 256), BF16),
        ((XP, 640, 256), BF16),
        ((XP, 256, 256), BF16),
        ((3, XP, 128, 256), BF16),
        ((XP, 128, 256), BF16),
        ((3, 2, XP, 24, 256), F32),
        ((2, 8, 32, 256), F32),
        ((XP, 32, 256), F32),
        ((3, 8, 8, 256), F32),
        ((256, 192), BF16),
        ((256, 384), BF16),
        ((384, 768), BF16),
        ((384, 768), BF16),
        ((192, 1536), BF16),
        ((1152, 256), F32),
        ((144, 256), F32),
        ((144, 128), F32),
        ((PACK_ROWS, 128), F32),
        ((16, 4 * ROWS, 128), BF16),
    ]
    return pl.pallas_call(
        main_kernel,
        out_shape=(
            jax.ShapeDtypeStruct((3, 2, 8, 128), F32),
            jax.ShapeDtypeStruct((4, 128, 128), BF16),
            jax.ShapeDtypeStruct((4, 64, 128), BF16),
            jax.ShapeDtypeStruct((4, 64, 128), BF16),
            jax.ShapeDtypeStruct((PACK_ROWS // 2, 128), F32),
            jax.ShapeDtypeStruct((PACK_ROWS // 2, 128), F32),
        ),
        in_specs=[pl.BlockSpec(memory_space=pltpu.HBM)] + [vmem()] * 8,
        out_specs=(vmem(),) * 6,
        scratch_shapes=[pltpu.VMEM(s, t) for s, t in scratch] + [pltpu.SemaphoreType.DMA],
        compiler_params=pltpu.CompilerParams(vmem_limit_bytes=56 * 1024 * 1024),
    )(noise, small, selector, taps2, taps2t, taps3, b1, b2, b3)


def window_kernel(copies, distant_ref, block_ref, paired_ref, across_ref, out_ref):
    me = lax.axis_index("gy")
    even = lax.rem(me, 2) == 0
    even_chip = lax.rem(me // 2, 2) == 0
    for x in range(2):
        before = jnp.where(even_chip, across_ref[x], paired_ref[x])
        after = jnp.where(even_chip, paired_ref[x], across_ref[x])
        tiles = [before[:8], before[8:], block_ref[x, :8], block_ref[x, 8:], after[:8], after[8:]]
        distant = distant_ref[x]
        rows = [jnp.where(even, distant, tiles[0])]
        rows += [jnp.where(even, tiles[k - 1], tiles[k]) for k in range(1, 6)]
        rows += [jnp.where(even, tiles[5], distant)]
        window = jnp.concatenate(rows, axis=0).astype(BF16)
        for k in range(copies):
            out_ref[k, x] = window


def run_window(distant, block, paired, across):
    copies = lax.axis_size("gx")
    return pl.pallas_call(
        functools.partial(window_kernel, copies),
        out_shape=jax.ShapeDtypeStruct((copies, 2, 4 * ROWS, 128), BF16),
        in_specs=[vmem()] * 4,
        out_specs=vmem(),
        compiler_params=pltpu.CompilerParams(vmem_limit_bytes=16 * 1024 * 1024),
    )(distant, block, paired, across)


def run_input(partner, beyond, own, taps, parts, noise):
    return pl.pallas_call(
        input_kernel,
        out_shape=(jax.ShapeDtypeStruct((2, 8, 128), F32),) * 2,
        in_specs=[vmem()] * 6,
        out_specs=(vmem(),) * 2,
        scratch_shapes=[pltpu.VMEM((48, 1024), BF16)],
        compiler_params=pltpu.CompilerParams(vmem_limit_bytes=16 * 1024 * 1024),
    )(partner, beyond, own, taps, parts, noise)


def unpack_kernel(scale, mine_ref, theirs_ref, loss, first, b1, middle, b2, last, b3, both):
    core = lax.rem(lax.axis_index("gy"), 2)
    half = PACK_ROWS // 2
    both[pl.ds(pl.multiple_of(core * half, 8), half), :] = mine_ref[...] * scale
    both[pl.ds(pl.multiple_of((1 - core) * half, 8), half), :] = theirs_ref[...] * scale

    def lanes_from(v, start):
        return v if start == 0 else pltpu.roll(v, 128 - start, 1)

    for d in range(3):
        for j in range(3):
            a = 2 - j
            g = d * 3 + j
            most = both[g * 16 : g * 16 + 16, :]
            third = both[144 + (g // 2) * 16 : 160 + (g // 2) * 16, :]
            for b in range(3):
                for c in range(3):
                    if b < 2:
                        v = lanes_from(most, b * 64 + c * 16)
                    else:
                        v = lanes_from(third, (g % 2) * 64 + c * 16)
                    middle[a * 27 + b * 9 + c * 3 + d] = v[:, :16]
    for d in range(3):
        for a in range(3):
            g = d * 3 + a
            if g < 8:
                v = lanes_from(both[224:240, :], 16 * g)
            else:
                v = lanes_from(both[208:224, :], 64)
            for b in range(3):
                for c in range(3):
                    row = b * 4 + c
                    first[a * 27 + b * 9 + c * 3 + d] = v[row : row + 1, :16]
    for b in range(3):
        for c in range(3):
            if b < 2:
                v = lanes_from(both[240:264, :], b * 64 + c * 16)
            else:
                v = lanes_from(both[264:288, :], c * 16)
            for d in range(3):
                for ch in range(2):
                    for a in range(3):
                        row = (2 - d) * 6 + ch * 3 + 2 - a
                        last[a * 27 + b * 9 + c * 3 + d, ch : ch + 1, :] = v[row : row + 1, :16]
    b2[...] = both[258:259, :16]
    b1[...] = both[259:260, :16]
    row = both[260:261, :]
    b3[...] = row[:, :2]
    loss[...] = pltpu.roll(row, 126, 1)[:, :1]


def run_unpack(scale, mine, theirs):
    shapes = ((1, 1), (81, 1, 16), (1, 16), (81, 16, 16), (1, 16), (81, 2, 16), (1, 2))
    return pl.pallas_call(
        functools.partial(unpack_kernel, scale),
        out_shape=tuple(jax.ShapeDtypeStruct(s, F32) for s in shapes),
        in_specs=[vmem(), vmem()],
        out_specs=(vmem(),) * len(shapes),
        scratch_shapes=[pltpu.VMEM((PACK_ROWS, 128), F32)],
        compiler_params=pltpu.CompilerParams(vmem_limit_bytes=16 * 1024 * 1024),
    )(mine, theirs)


def pad_taps(v):
    return jnp.pad(v, [(0, 0)] * (v.ndim - 2) + [(0, 1), (0, 0)])


def taps_kernel(kernel_ref, taps_ref, flipped_ref, spread):
    shape = (16, 128)
    lane = iota(shape, 1)
    group = (lane // 16) % 4
    repeat = jnp.where(iota(shape, 0) == lane % 16, 1.0, 0.0).astype(BF16)
    spread[...] = jnp.dot(kernel_ref[...], repeat, preferred_element_type=F32)
    unit = jnp.where(iota((16, 16), 0) == iota((16, 16), 1), 1.0, 0.0).astype(BF16)
    starts = [128 * k for k in range(10)] + [1168]
    turned = [
        lax.dot_general(
            unit, kernel_ref[k : k + 128, :], (((1,), (1,)), ((), ())), preferred_element_type=F32
        )
        for k in starts
    ]
    zero = jnp.zeros(shape, F32)
    for d in range(3):
        for a in range(3):
            for b in range(3):
                plain = zero
                flipped = zero
                for c in range(3):
                    tap = a * 27 + b * 9 + c * 3 + d
                    plain = jnp.where(group == c, spread[tap * 16 : tap * 16 + 16, :], plain)
                    tap = 80 - tap
                    chunk = tap // 8
                    offset = tap * 16 - starts[chunk]
                    shift = (c * 16 - offset) % 128
                    v = turned[chunk]
                    v = pltpu.roll(v, shift, 1) if shift else v
                    flipped = jnp.where(lane // 16 == c, v, flipped)
                flipped = flipped + pltpu.roll(flipped, 64, 1)
                taps_ref[d * 9 + a * 3 + b] = plain.astype(BF16)
                flipped_ref[d * 9 + a * 3 + b] = flipped.astype(BF16)


def hidden_taps(kernel):
    return pl.pallas_call(
        taps_kernel,
        out_shape=(jax.ShapeDtypeStruct((27, 16, 128), BF16),) * 2,
        in_specs=[vmem()],
        out_specs=(vmem(),) * 2,
        scratch_shapes=[pltpu.VMEM((1296, 128), F32)],
        compiler_params=pltpu.CompilerParams(vmem_limit_bytes=16 * 1024 * 1024),
    )(jnp.transpose(kernel, (2, 3, 4, 5, 0, 1)).reshape(1296, 16))


def banded_taps(v):
    v = pad_taps(v)
    v = jnp.stack([jnp.roll(v, t - 1, axis=2) for t in range(4)], axis=2)
    v = v.reshape(27, -1, 64)
    return jnp.concatenate([v, v], axis=2)


def swapped(v, axis_size, partner):
    return lax.ppermute(v, "gy", [(i, partner(i)) for i in range(axis_size)])


def gather_y(noise, weights):
    size_y = lax.axis_size("gy")
    even = lax.axis_index("gy") % 2 == 0
    chips = size_y // 2

    def far(i):
        return (i - 3) % size_y if i % 2 == 0 else (i + 3) % size_y

    def chip_after(i):
        return ((((i >> 1) + 1) ^ 1) - 1) % chips * 2 + (i & 1)

    distant = swapped(noise, size_y, far)
    beside = swapped(noise, size_y, lambda i: i ^ 1)
    block = jnp.concatenate(
        [jnp.where(even, noise, beside), jnp.where(even, beside, noise)], axis=1
    )
    block, *weights = lax.optimization_barrier((block, *weights))
    paired = swapped(block, size_y, lambda i: i ^ 2)
    across = swapped(block, size_y, chip_after)
    return run_window(
        distant.reshape(2, 8, 128),
        block.reshape(2, 16, 128),
        paired.reshape(2, 16, 128),
        across.reshape(2, 16, 128),
    ), weights


def sum_over_y(mine, theirs, *before_last):
    size_y = lax.axis_size("gy")

    def along_z(partner):
        def f(i):
            return ((i >> 4) * 8 + partner((i >> 1) & 7)) * 2 + (i & 1)

        return f

    crossing = (3, 6, 5, 0, 7, 2, 1, 4)
    v = mine + swapped(theirs, size_y, lambda i: i ^ 1)
    for partner in (
        lambda i: i ^ 16,
        along_z(lambda z: z ^ 1),
        along_z(lambda z: (((z + 1) ^ 1) - 1) % 8),
    ):
        v = v + swapped(v, size_y, partner)
    v, *before_last = lax.optimization_barrier((v, *before_last))
    v = v + swapped(v, size_y, along_z(lambda z: crossing[z]))
    return v, before_last


def local(noise, w_first, b_first, w_middle, b_middle, w_last, b_last):
    size_y = lax.axis_size("gy")
    sites = float(noise.size * lax.axis_size("gx") * size_y)
    sent, (w_first, w_middle, w_last) = gather_y(noise, (w_first, w_middle, w_last))
    gathered = lax.all_to_all(sent, "gx", 0, 0, tiled=True).reshape(16, 4 * ROWS, 128)
    flip = (slice(None), slice(None)) + (slice(None, None, -1),) * 4
    small = jnp.concatenate(
        [
            jnp.transpose(w_first[:, 0], (4, 0, 1, 2, 3)).reshape(48, 27),
            jnp.transpose(w_last[flip], (5, 0, 1, 2, 3, 4)).reshape(96, 27),
        ],
        axis=0,
    )
    small = jnp.pad(small, ((0, 0), (0, 5)))
    taps2, taps2t = hidden_taps(w_middle)
    taps3 = banded_taps(jnp.transpose(w_last, (5, 2, 3, 0, 4, 1)).reshape(27, 2, 3, 16))
    tapsd = banded_taps(jnp.transpose(w_first[flip], (5, 2, 3, 1, 4, 0)).reshape(27, 1, 3, 16))
    tapsd = jnp.concatenate([tapsd, tapsd], axis=1)

    parts, window, to_partner, to_beyond, mine, theirs = run_main(
        gathered,
        small,
        jnp.asarray(tap_selector(), BF16),
        taps2,
        taps2t,
        taps3,
        b_first.reshape(1, 16),
        b_middle.reshape(1, 16),
        b_last.reshape(1, 2),
    )
    partner = swapped(to_partner, size_y, lambda i: i ^ 1)
    beyond = swapped(to_beyond, size_y, lambda i: (((i + 1) ^ 1) - 1) % size_y)
    mine, (partner, beyond) = sum_over_y(mine, theirs, partner, beyond)
    field, noise_grad = run_input(partner, beyond, window, tapsd, parts, noise.reshape(2, 8, 128))
    mine, field, noise_grad = lax.optimization_barrier((mine, field, noise_grad))
    theirs = swapped(mine, size_y, lambda i: i ^ 1)
    loss, first, b1, middle, b2, last, b3 = run_unpack(1.0 / sites, mine, theirs)
    return (
        field.reshape(noise.shape),
        noise_grad.reshape(noise.shape),
        loss.reshape(()),
        jnp.transpose(first.reshape(3, 3, 3, 3, 1, 16), (5, 4, 0, 1, 2, 3)),
        b1.reshape(16),
        jnp.transpose(middle.reshape(3, 3, 3, 3, 16, 16), (4, 5, 0, 1, 2, 3)),
        b2.reshape(16),
        jnp.transpose(last.reshape(3, 3, 3, 3, 2, 16), (4, 5, 0, 1, 2, 3)),
        b3.reshape(2),
    )


def solution(mesh):
    placed = (P("gx", "gy", None, None), P(), P(), P(), P(), P(), P())
    return jax.shard_map(
        local,
        mesh=mesh,
        in_specs=placed,
        out_specs=(P("gx", "gy", None, None), P("gx", "gy", None, None)) + (P(),) * 7,
        check_vma=False,
    )
```
